32 devices in a mesh: wide: 4 (over y, core), col: 8 (over z, x).
Axes of the slice: x: 2, y: 2, z: 4, core: 2. Of those that a mesh axis runs over, the one named last changes fastest.
Arguments:
- rhs: float32 [24576, 256], P(('wide', 'col')), may hold values from -6 to 6
- basis: bfloat16 [24576, 256], P(('wide', 'col')), may hold values from -0.21875 to 0.21875
- self_block: bfloat16 [24576, 768], P(('wide', 'col'))
- near_block: bfloat16 [32, 8, 768, 768], P(('wide', 'col')), may hold values from -0.0546875 to 0.0546875
- near_ids: int32 [32, 8], P(('wide', 'col')), may hold values from -1 to 31, as said below
- couplings: bfloat16 [32, 40, 256, 256], P(('wide', 'col')), may hold values from -0.09375 to 0.09375
- far_ids: int32 [32, 40], P(('wide', 'col')), may hold values from -1 to 31, as said below
- intersection_start: int32 [32, 2], P(('wide', 'col')), may hold values from 0 to 512
- schwarz_inverse: bfloat16 [32, 1280, 1280], P(('wide', 'col'))
Outputs:
- solution: float32 [24576, 256], P(('wide', 'col'))
The draws below stay inside these ranges and needn't reach their ends.
Inputs may be any that keep to these rules, and one draw needn't show every extreme that they name: `near_ids`: row c lists every cluster adjacent to cluster c on the grid (larger index distance 1; id = first index * 8 + second), ids first and -1 after them; rows of corner and edge clusters end in -1. `far_ids`: row c lists distinct clusters whose larger grid index distance from cluster c is 2 to 3, ids first and -1 after them; counts are ragged, and some rows list every such cluster. `intersection_start`: column 0 starts the rows taken by the domain of the cluster before along the second grid index, column 1 those taken by the one after.
All inputs are finite; a program needn't handle non-finite values.
Results may differ from the reference program's by a relative error of at most 0.0025.
The reference program's roundings to bfloat16 on the way count: a program that leaves them out, or rounds other values in their place, can miss the bound.
Values may be sent and summed in bfloat16 or wider, within the bound.
No kernel may reach another device: no remote copies, remote signals or barrier semaphores. Data moves between devices by JAX's collectives and lax.ppermute only.
A program may use at most 128 MiB of HBM per device.

```python
import math
import jax
import jax.numpy as jnp
import numpy as np
from jax import lax

M = 768
K = 256
R = 256
OV = 256
REACH = 3
NEAR = 8
ITERS = 2
LMAX = 40
ORDER = 1280
WIDE_CLUSTERS = 4
COL_CLUSTERS = 8
CLUSTERS = 32
ROWS = 24576


def draw_self_block(key, part):
    row_pos = jnp.arange(ROWS)[:, None] % M
    col_pos = jnp.arange(M)[None, :]
    identity = (row_pos == col_pos).astype(jnp.float32)
    noise = 0.5 * jax.random.normal(key, (ROWS, M), jnp.float32) / math.sqrt(M)
    diag_scale = 2.0
    return (noise + diag_scale * identity).astype(jnp.bfloat16)


def draw_schwarz_inverse(key, part):
    identity = jnp.eye(ORDER, dtype=jnp.float32)[None]
    noise = 0.3 * jax.random.normal(key, (CLUSTERS, ORDER, ORDER), jnp.float32) / math.sqrt(ORDER)
    return (noise + identity).astype(jnp.bfloat16)


def grid_candidates(offsets):
    cluster_ids = jnp.arange(CLUSTERS)
    wide_pos = cluster_ids // COL_CLUSTERS
    col_pos = cluster_ids % COL_CLUSTERS
    steps_arr = jnp.asarray(offsets, jnp.int32)
    new_wide = wide_pos[:, None] + steps_arr[None, :, 0]
    new_col = col_pos[:, None] + steps_arr[None, :, 1]
    inside = (new_wide >= 0) & (new_wide < WIDE_CLUSTERS) & (new_col >= 0) & (new_col < COL_CLUSTERS)
    return (new_wide * COL_CLUSTERS + new_col, inside)


def draw_near_ids(key, part):
    offsets = np.array([(a, b) for a in range(-1, 2) for b in range(-1, 2) if not (a == 0 and b == 0)], np.int32)
    count_all = offsets.shape[0]
    candidates, inside = grid_candidates(offsets)
    scores = jax.random.randint(key, (CLUSTERS, count_all), 0, 1 << 20) * 8 + jnp.arange(count_all)
    scores = jnp.where(inside, scores, -1 - jnp.arange(count_all))
    top_scores, order = lax.top_k(scores, NEAR)
    picked = jnp.take_along_axis(candidates, order, axis=1)
    return jnp.where(top_scores >= 0, picked, -1).astype(jnp.int32)


def draw_far_ids(key, part):
    offsets = np.array([(a, b) for a in range(-REACH, REACH + 1) for b in range(-REACH, REACH + 1) if max(abs(a), abs(b)) >= 2], np.int32)
    candidates, inside = grid_candidates(offsets)
    key_scores = jax.random.fold_in(key, 11)
    key_count = jax.random.fold_in(key, 12)
    key_hot = jax.random.fold_in(key, 13)
    scores = jax.random.randint(key_scores, (CLUSTERS, LMAX), 0, 1 << 20) * 64 + jnp.arange(LMAX)
    scores = jnp.where(inside, scores, -1 - jnp.arange(LMAX))
    top_scores, order = lax.top_k(scores, LMAX)
    picked = jnp.take_along_axis(candidates, order, axis=1)
    live_total = jnp.sum(inside.astype(jnp.int32), axis=1)
    drawn_count = jax.random.randint(key_count, (CLUSTERS,), 4, 24)
    is_hot = jax.random.randint(key_hot, (CLUSTERS,), 0, 8) == 0
    cluster_ids = jnp.arange(CLUSTERS)
    middle = cluster_ids == WIDE_CLUSTERS // 2 * COL_CLUSTERS + COL_CLUSTERS // 2
    counts = jnp.where(is_hot | middle, live_total, jnp.minimum(drawn_count, live_total))
    ranks = jnp.arange(LMAX)[None, :]
    return jnp.where(ranks < counts[:, None], picked, -1).astype(jnp.int32)


def plant(values, own_key, smallest, top_value):
    longest = values.shape.index(max(values.shape))
    spots = []
    for shift in (0, 1):
        where = [jax.random.randint(jax.random.fold_in(own_key, axis), (), 0, length) for axis, length in enumerate(values.shape)]
        where[longest] = (where[longest] + shift) % values.shape[longest]
        spots.append(tuple(where))
    return values.at[spots[0]].set(smallest).at[spots[1]].set(top_value)


def block_scale(key, shape, shards, smallest, largest):
    level, own = 1.0, jax.random.fold_in(key, 6)
    for dim, parts in shards:
        draws = jnp.exp(jax.random.uniform(jax.random.fold_in(own, dim), (parts,), jnp.float32, smallest / len(shards), largest / len(shards)))
        level = level * jnp.repeat(draws, shape[dim] // parts).reshape([-1 if axis == dim else 1 for axis in range(len(shape))])
    return level


def bell_draw(key, extent, deviation, most, pieces=(), held_as=jnp.bfloat16):
    gain = block_scale(key, extent, pieces, -0.22, 0.18) if pieces else 1.0
    values = jax.random.normal(key, extent, jnp.float32) * deviation * gain
    return jnp.minimum(jnp.maximum(values, -most), most).astype(held_as)


def setup_inputs(seed: int = 0) -> dict:
    streams_of = jax.random.split(jax.random.key(seed), 10)
    rhs = bell_draw(streams_of[0], (ROWS, K), 1.0, 6.0, ((0, 32),), jnp.float32)
    basis = bell_draw(streams_of[1], (ROWS, R), M ** -0.5, 0.21875, ((0, 32),))
    self_block = draw_self_block(jax.random.fold_in(streams_of[9], 71), 0)
    near_block = bell_draw(streams_of[3], (CLUSTERS, NEAR, M, M), (16 * M) ** -0.5, 0.0546875, ((0, 32),))
    near_ids = draw_near_ids(jax.random.fold_in(streams_of[9], 71), 0)
    couplings = bell_draw(streams_of[5], (CLUSTERS, LMAX, R, R), (16 * R) ** -0.5, 0.09375, ((0, 32),))
    far_ids = draw_far_ids(jax.random.fold_in(streams_of[9], 71), 0)
    intersection_start = plant(jax.random.randint(streams_of[7], (CLUSTERS, 2), 0, M - OV + 1), jax.random.fold_in(streams_of[7], 1), 0, M - OV).astype(jnp.int32)
    schwarz_inverse = draw_schwarz_inverse(jax.random.fold_in(streams_of[9], 71), 0)
    return {"rhs": rhs, "basis": basis, "self_block": self_block, "near_block": near_block, "near_ids": near_ids, "couplings": couplings, "far_ids": far_ids, "intersection_start": intersection_start, "schwarz_inverse": schwarz_inverse}


HIGHEST_PREC = lax.Precision.HIGHEST

def gram_of(left, right):
    return jnp.einsum('nk,nj->kj', left, right, precision=HIGHEST_PREC)

def lower_solve(factor, matrix):
    return lax.linalg.triangular_solve(factor, matrix, left_side=False, lower=True, transpose_a=True)

def apply_operator(vector_in, basis, self_block, near_block, near_ids, couplings, far_ids):
    rounded = vector_in.astype(jnp.bfloat16).reshape(CLUSTERS, M, K)
    basis_c = basis.reshape(CLUSTERS, M, R)
    self_c = self_block.reshape(CLUSTERS, M, M)
    coefficients = jnp.einsum('cmr,cmk->crk', basis_c.astype(jnp.float32), rounded.astype(jnp.float32)).astype(jnp.bfloat16)

    def one_cluster(inputs):
        self_m, near_m, near_row, coupling_row, far_row, basis_m, own_vec = inputs
        result = jnp.dot(self_m.astype(jnp.float32), own_vec.astype(jnp.float32), preferred_element_type=jnp.float32)
        for slot_index in range(NEAR):
            neighbour = near_row[slot_index]
            other = rounded[jnp.maximum(neighbour, 0)]
            product = jnp.dot(near_m[slot_index].astype(jnp.float32), other.astype(jnp.float32), preferred_element_type=jnp.float32)
            result = result + jnp.where(neighbour >= 0, product, jnp.zeros_like(product))
        picked = coefficients[jnp.maximum(far_row, 0)]
        weighted = jnp.where((far_row >= 0)[:, None, None], coupling_row, jnp.zeros_like(coupling_row))
        far_sum = jnp.einsum('lrs,lsk->rk', weighted.astype(jnp.float32), picked.astype(jnp.float32))
        result = result + jnp.dot(basis_m.astype(jnp.float32), far_sum.astype(jnp.bfloat16).astype(jnp.float32), preferred_element_type=jnp.float32)
        return result
    outcome = lax.map(one_cluster, (self_c, near_block, near_ids, couplings, far_ids, basis_c, rounded))
    return outcome.reshape(ROWS, K)

def precondition(vector_in, intersection_start, schwarz_inverse):
    rounded = vector_in.astype(jnp.bfloat16).reshape(CLUSTERS, M, K)
    position = jnp.arange(CLUSTERS) % COL_CLUSTERS
    has_prev = (position > 0)[:, None, None]
    has_next = (position < COL_CLUSTERS - 1)[:, None, None]

    def window(matrix, start):
        return lax.dynamic_slice_in_dim(matrix, start, OV, 0)
    bottoms = jax.vmap(window)(rounded, intersection_start[:, 1])
    tops = jax.vmap(window)(rounded, intersection_start[:, 0])
    prev_rows = jnp.where(has_prev, jnp.roll(bottoms, 1, axis=0), jnp.zeros_like(bottoms))
    next_rows = jnp.where(has_next, jnp.roll(tops, -1, axis=0), jnp.zeros_like(tops))
    domain = jnp.concatenate([prev_rows, rounded, next_rows], axis=1)
    solved = lax.map(lambda pair: jnp.dot(pair[0].astype(jnp.float32), pair[1].astype(jnp.float32), preferred_element_type=jnp.float32), (schwarz_inverse, domain))
    result = solved[:, OV:OV + M]
    to_prev = solved[:, :OV]
    to_next = solved[:, OV + M:]
    from_next = jnp.where(has_next, jnp.roll(to_prev, -1, axis=0), jnp.zeros_like(to_prev))
    from_prev = jnp.where(has_prev, jnp.roll(to_next, 1, axis=0), jnp.zeros_like(to_next))

    def place(matrix, addend, start):
        current = lax.dynamic_slice_in_dim(matrix, start, OV, 0)
        return lax.dynamic_update_slice_in_dim(matrix, current + addend, start, 0)
    result = jax.vmap(place)(result, from_next, intersection_start[:, 1])
    result = jax.vmap(place)(result, from_prev, intersection_start[:, 0])
    return result.reshape(ROWS, K)

def reference(rhs, basis, self_block, near_block, near_ids, couplings, far_ids, intersection_start, schwarz_inverse):
    factor = jnp.linalg.cholesky(gram_of(rhs, rhs))
    beta_block = factor.T
    bases = [lower_solve(factor, rhs)]
    directions = []
    columns = []
    for iteration in range(ITERS):
        precond_out = precondition(bases[-1], intersection_start, schwarz_inverse)
        image = apply_operator(precond_out, basis, self_block, near_block, near_ids, couplings, far_ids)
        stacked = jnp.concatenate(bases, axis=1)
        projected = gram_of(stacked, image)
        image = image - jnp.dot(stacked, projected, precision=HIGHEST_PREC)
        factor = jnp.linalg.cholesky(gram_of(image, image))
        columns.append((projected, factor.T))
        directions.append(precond_out)
        if iteration + 1 < ITERS:
            bases.append(lower_solve(factor, image))
    hessen = jnp.zeros(((ITERS + 1) * K, ITERS * K), jnp.float32)
    for column_index, (projected, sub_block) in enumerate(columns):
        upper_rows = (column_index + 1) * K
        hessen = hessen.at[:upper_rows, column_index * K:(column_index + 1) * K].set(projected)
        hessen = hessen.at[upper_rows:upper_rows + K, column_index * K:(column_index + 1) * K].set(sub_block)
    normal_matrix = jnp.dot(hessen.T, hessen, precision=HIGHEST_PREC)
    target = jnp.dot(hessen[:K].T, beta_block, precision=HIGHEST_PREC)
    small_factor = jnp.linalg.cholesky(normal_matrix)
    middle = lax.linalg.triangular_solve(small_factor, target, left_side=True, lower=True)
    weights_y = lax.linalg.triangular_solve(small_factor, middle, left_side=True, lower=True, transpose_a=True)
    return jnp.dot(jnp.concatenate(directions, axis=1), weights_y, precision=HIGHEST_PREC)
```

```python
import functools

import jax
import jax.numpy as jnp
from jax import lax
from jax.experimental import pallas as pl
from jax.experimental.pallas import tpu as pltpu
from jax.sharding import PartitionSpec as P

REACH = 3
ITERS = 2
HIGHEST_PREC = lax.Precision.HIGHEST
SUB = 8
LANES = 128


def send(block, axis, route):
    return lax.ppermute(block, axis, route)


def along(block, axis, distance):
    count = lax.axis_size(axis)
    return send(
        block, axis, [(i, i + distance) for i in range(count) if 0 <= i + distance < count]
    )


def swap(block, axis, bit):
    return send(block, axis, [(i, i ^ bit) for i in range(lax.axis_size(axis))])


def outward(block, axis):
    count = lax.axis_size(axis)
    route = [(i, i + 1 if i % 2 else i - 1) for i in range(count)]
    return send(block, axis, [(s, t) for s, t in route if 0 <= t < count])


def relay(block, axis):
    count = lax.axis_size(axis)
    route = [(i, i - 2 if i % 2 else i + 2) for i in range(count)]
    return send(block, axis, [(s, t) for s, t in route if 0 <= t < count])


def is_even(axis):
    return lax.axis_index(axis) % 2 == 0


def split_sum(block, axis, bit):
    half = block.shape[0] // 2
    mine = (lax.axis_index(axis) // bit) % 2
    kept = lax.dynamic_slice_in_dim(block, mine * half, half, 0)
    given = lax.dynamic_slice_in_dim(block, (1 - mine) * half, half, 0)
    return kept + swap(given, axis, bit)


def join_halves(block, axis, bit):
    mine = (lax.axis_index(axis) // bit) % 2
    other = swap(block, axis, bit)
    return jnp.where(
        mine == 0,
        jnp.concatenate([block, other], axis=0),
        jnp.concatenate([other, block], axis=0),
    )


def is_power_of_two(count):
    return count & (count - 1) == 0


def sum_everywhere(block, splits):
    sizes = (lax.axis_size("wide"), lax.axis_size("col"))
    if not all(is_power_of_two(size) for size in sizes):
        return lax.psum(block, ("wide", "col"))
    stages = []
    for axis, size in zip(("wide", "col"), sizes):
        bit = 1
        while bit < size:
            stages.append((axis, bit))
            bit *= 2
    split_stages = stages[:splits]
    for axis, bit in split_stages:
        block = split_sum(block, axis, bit)
    for axis, bit in stages[splits:]:
        block = block + swap(block, axis, bit)
    for axis, bit in reversed(split_stages):
        block = join_halves(block, axis, bit)
    return block


def far_line(block, axis):
    rows = block.shape[0]
    pair = swap(block, axis, 1)
    both = jnp.concatenate([block, pair], axis=0)
    below = along(both, axis, 2)
    above = along(both, axis, -2)
    last = relay(jnp.where(is_even(axis), below[rows:], above[rows:]), axis)
    return [
        (block, 0),
        (pair, 0),
        (below, 0),
        (below, 1),
        (above, 0),
        (above, 1),
        (last, 0),
    ]


def line_slot(target, own):
    pair_step = target // 2 - own // 2
    other = (target + own) % 2
    return jnp.where(
        pair_step == 0,
        other,
        jnp.where(pair_step == -1, 2 + other, jnp.where(pair_step == 1, 4 + other, 6)),
    )


def near_slot(target, own):
    return jnp.where(target == own, 0, jnp.where(target // 2 == own // 2, 1, 2))


def short_wide():
    return lax.axis_size("wide") == REACH + 1


def far_row_slot(target, own, short):
    if short:
        same_pair = target // 2 == own // 2
        other = (target + own) % 2
        return jnp.where(same_pair, 0, 2) + other
    return line_slot(target, own)


def gather_windows(zb, coef):
    xc = swap(coef, "col", 1)
    xn = swap(zb, "col", 1)
    rank = coef.shape[0]
    pair = jnp.concatenate([coef, xc], axis=0)
    zu = along(pair, "col", 2)
    zd = along(pair, "col", -2)
    zn = relay(xn, "col")
    third = relay(jnp.where(is_even("col"), zu[rank:], zd[rank:]), "col")
    own_line = [(coef, 0), (xc, 0), (zu, 0), (zu, 1), (zd, 0), (zd, 1), (third, 0)]
    near = {}
    for col_slot, piece in enumerate((zb, xn, zn)):
        near[0, col_slot] = piece
        near[1, col_slot] = swap(piece, "wide", 1)
        near[2, col_slot] = outward(piece, "wide")
    far = {}
    if short_wide():
        yc0 = swap(coef, "wide", 2)
        yc1 = swap(xc, "wide", 2)
        yc2 = swap(jnp.concatenate([zu, zd], axis=0), "wide", 2)
        yc3 = swap(third, "wide", 2)
        ca = swap(jnp.concatenate([coef, xc, yc0, yc1], axis=0), "wide", 1)
        cb = swap(jnp.concatenate([zu, zd, yc2], axis=0), "wide", 1)
        cc = swap(jnp.concatenate([third, yc3], axis=0), "wide", 1)
        y_line = [(yc0, 0), (yc1, 0), (yc2, 0), (yc2, 1), (yc2, 2), (yc2, 3), (yc3, 0)]
        c_line = [(ca, 0), (ca, 1), (cb, 0), (cb, 1), (cb, 2), (cb, 3), (cc, 0)]
        cy_line = [(ca, 2), (ca, 3), (cb, 4), (cb, 5), (cb, 6), (cb, 7), (cc, 1)]
        for wide_slot, line in enumerate((own_line, c_line, y_line, cy_line)):
            for col_slot, piece in enumerate(line):
                far[wide_slot, col_slot] = piece
    else:
        stacked = jnp.concatenate([coef, xc, zu, zd, third], axis=0)
        for wide_slot, (array, part) in enumerate(far_line(stacked, "wide")):
            for col_slot in range(2 * REACH + 1):
                far[wide_slot, col_slot] = (array, part * (2 * REACH + 1) + col_slot)
    return near, far


def mm(left, right, contract=(1, 0)):
    return lax.dot_general(
        left,
        right,
        (((contract[0],), (contract[1],)), ((), ())),
        precision=HIGHEST_PREC,
        preferred_element_type=jnp.float32,
    )


def mm_bf16(left, right, contract=(1, 0)):
    return lax.dot_general(
        left,
        right,
        (((contract[0],), (contract[1],)), ((), ())),
        preferred_element_type=jnp.float32,
    )


def row_across(tile, row):
    return jnp.broadcast_to(tile[row : row + 1, :], tile.shape)


def eliminate_strip(strip, pivots):
    rows = lax.broadcasted_iota(jnp.int32, (SUB, LANES), 0)
    columns = [
        jnp.broadcast_to(strip[:, pivots + j : pivots + j + 1], (SUB, LANES)) for j in range(SUB)
    ]
    tiles = [strip[:, t : t + LANES] for t in range(0, strip.shape[1], LANES)]
    for i in range(SUB):
        inverse_root = lax.rsqrt(row_across(columns[i], i))
        factor = jnp.where(rows > i, columns[i] * inverse_root, 0.0)
        for j in range(i + 1, SUB):
            columns[j] = columns[j] - factor * (row_across(columns[j], i) * inverse_root)
        for t in range(len(tiles)):
            scaled = row_across(tiles[t], i) * inverse_root
            tiles[t] = jnp.where(rows == i, scaled, tiles[t] - factor * scaled)
    return jnp.concatenate(tiles, axis=1)


def factorize(work):
    size = work.shape[0]
    work[:, size:] = (
        lax.broadcasted_iota(jnp.int32, (size, size), 0)
        == lax.broadcasted_iota(jnp.int32, (size, size), 1)
    ).astype(jnp.float32)
    for first in range(0, size, LANES):
        lanes = slice(first, size + first + LANES)
        for top in range(first, first + LANES, SUB):
            strip = eliminate_strip(work[top : top + SUB, lanes], top - first)
            work[top : top + SUB, lanes] = strip
            turned = strip[:, :LANES].T
            for row in range(top + SUB, first + LANES, SUB):
                block = turned[row - first : row - first + SUB, :]
                rest = work[row : row + SUB, lanes]
                for i in range(SUB):
                    rest = rest - jnp.broadcast_to(block[:, i : i + 1], rest.shape) * jnp.broadcast_to(
                        strip[i : i + 1, :], rest.shape
                    )
                work[row : row + SUB, lanes] = rest
        if first + LANES < size:
            done = work[first : first + LANES, lanes]
            for row in range(first + LANES, size, LANES):
                update = mm(done[:, row - first : row - first + LANES], done, (0, 0))
                work[row : row + LANES, lanes] = work[row : row + LANES, lanes] - update


def upper(work):
    size = work.shape[0]
    keep = lax.broadcasted_iota(jnp.int32, (size, size), 1) >= lax.broadcasted_iota(
        jnp.int32, (size, size), 0
    )
    return jnp.where(keep, work[:, :size], 0.0)


def window_rows(padded, start, size):
    base = pl.multiple_of((start // SUB) * SUB, SUB)
    taken = padded[pl.ds(base, size + SUB), :]
    return pltpu.roll(taken, (size + SUB - start % SUB) % (size + SUB), 0)[:size]


def add_window(padded, start, addend):
    size = addend.shape[0]
    base = pl.multiple_of((start // SUB) * SUB, SUB)
    longer = jnp.concatenate([addend, jnp.zeros((SUB, addend.shape[1]), addend.dtype)], axis=0)
    span = pl.ds(base, size + SUB)
    padded[span, :] = padded[span, :] + pltpu.roll(longer, start % SUB, 0)


def write_vector(vector, starts, v_out, vb_out, top_out, bottom_out, padded):
    rows = vector.shape[0]
    v_out[...] = vector
    vb_out[...] = vector.astype(jnp.bfloat16)
    padded[:rows, :] = vector
    padded[rows:, :] = jnp.zeros((SUB, vector.shape[1]), vector.dtype)
    margin = top_out.shape[0]
    top_out[...] = window_rows(padded, starts[0, 0], margin).astype(jnp.bfloat16)
    bottom_out[...] = window_rows(padded, starts[0, 1], margin).astype(jnp.bfloat16)


def first_kernel(starts, gram, rhs, v_out, vb_out, top_out, bottom_out, u_out, c11_out, work, padded):
    size = gram.shape[0]
    work[:, :size] = gram[...]
    factorize(work)
    inverse = work[:, size:]
    write_vector(mm(rhs[...], inverse, (1, 1)), starts, v_out, vb_out, top_out, bottom_out, padded)
    u_out[...] = upper(work)
    c11_out[...] = mm(mm(inverse, gram[...]), inverse, (1, 1))


def second_kernel(
    starts, sums, c11, v1, w, v_out, vb_out, top_out, bottom_out, u_out, inv_out, gram_out, work, padded
):
    size = c11.shape[0]
    h = sums[:, :size]
    gram = sums[:, size:] - mm(h, 2.0 * h - mm(c11[...], h), (0, 0))
    gram_out[...] = gram
    work[:, :size] = gram
    factorize(work)
    inverse = work[:, size:]
    rest = w[...] - mm(v1[...], h)
    write_vector(mm(rest, inverse, (1, 1)), starts, v_out, vb_out, top_out, bottom_out, padded)
    u_out[...] = upper(work)
    inv_out[...] = inverse


def third_kernel(sums, c11, u0, inv1, gram1, k_inv_out, t1_out, c12_out, c22_out, work):
    size = c11.shape[0]
    h = sums[:, :size]
    left = mm(c11[...], h)
    work[:, :size] = sums[:, size:] + mm(h, left - h, (0, 0))
    factorize(work)
    k_inverse = work[:, size:]
    k_inv_out[...] = k_inverse
    t1_out[...] = mm(k_inverse, mm(h, u0[...], (0, 0)))
    c12_out[...] = mm(h - left, inv1[...], (1, 1))
    c22_out[...] = mm(mm(inv1[...], gram1[...]), inv1[...], (1, 1))


def last_kernel(
    sums2, sums1, c11, c12, c22, u0, u1, k_inv, t1, z1, z2, out, work
):
    size = c11.shape[0]
    h11 = sums1[:, :size]
    h12 = sums2[:, :size]
    h22 = sums2[:, size : 2 * size]
    extra1 = mm(c11[...], h12) + mm(c12[...], h22) - h12
    extra2 = mm(c12[...], h12, (0, 0)) + mm(c22[...], h22) - h22
    n22 = sums2[:, 2 * size :] + mm(h12, extra1, (0, 0)) + mm(h22, extra2, (0, 0))
    n12 = mm(h11, h12, (0, 0)) + mm(u1[...], h22, (0, 0))
    cross = mm(k_inv[...], n12)
    work[:, :size] = n22 - mm(cross, cross, (0, 0))
    factorize(work)
    inverse = work[:, size:]
    t2 = mm(inverse, mm(h12, u0[...], (0, 0)) - mm(cross, t1[...], (0, 0)))
    y2 = mm(inverse, t2, (0, 0))
    y1 = mm(k_inv[...], t1[...] - mm(cross, y2), (0, 0))
    out[...] = mm(z1[...], y1) + mm(z2[...], y2)


def schwarz_kernel(inverse, centre, before, after, low_out, high_out, mid_out):
    margin = before.shape[0]
    rows = centre.shape[0] - 2 * margin
    solved = (
        centre[...]
        + mm_bf16(inverse[0, :, :margin], before[...])
        + mm_bf16(inverse[0, :, margin + rows :], after[...])
    )
    low_out[...] = solved[:margin]
    mid_out[...] = solved[margin : margin + rows]
    high_out[...] = solved[margin + rows :]


def place_kernel(starts, mid, from_next, from_prev, basis, z_out, zb_out, coef_out, padded):
    rows = mid.shape[0]
    padded[:rows, :] = mid[...]
    padded[rows:, :] = jnp.zeros((SUB, mid.shape[1]), jnp.float32)
    add_window(padded, starts[0, 1], from_next[...])
    add_window(padded, starts[0, 0], from_prev[...])
    z = padded[:rows, :]
    z_out[...] = z
    zb = z.astype(jnp.bfloat16)
    zb_out[...] = zb
    coef_out[...] = mm_bf16(basis[...], zb, (0, 0)).astype(jnp.bfloat16)


def in_vmem():
    return pl.BlockSpec(memory_space=pltpu.VMEM)


def in_smem():
    return pl.BlockSpec(memory_space=pltpu.SMEM)


def call(kernel, shapes, smem, args, scratch=()):
    specs = [in_smem() if i in smem else in_vmem() for i in range(len(args))]
    outs = tuple(jax.ShapeDtypeStruct(shape, dtype) for shape, dtype in shapes)
    return pl.pallas_call(
        kernel,
        out_shape=outs,
        in_specs=specs,
        out_specs=tuple(in_vmem() for _ in outs),
        scratch_shapes=list(scratch),
        name=kernel.__name__,
    )(*args)


def operator_kernel(*refs, near_count, far_places, n_far, n_vectors, short):
    it = iter(refs)
    near_ids, far_ids, place = next(it), next(it), next(it)
    near_hbm = [next(it) for _ in range(near_count)]
    far_hbm = [next(it) for _ in range(n_far)]
    self_hbm, blocks_hbm, couplings_hbm, basis_hbm = (next(it) for _ in range(4))
    vectors_hbm = [next(it) for _ in range(n_vectors)]
    w_out, sums_out = next(it), next(it)
    near = [next(it) for _ in range(near_count)]
    far = [next(it) for _ in range(n_far)]
    self_block, blocks, couplings, basis = (next(it) for _ in range(4))
    vectors = [next(it) for _ in range(n_vectors)]
    near_table, far_table, sems = next(it), next(it), next(it)

    sources = [self_hbm] + near_hbm + [blocks_hbm] + far_hbm + [couplings_hbm, basis_hbm]
    targets = [self_block] + near + [blocks] + far + [couplings, basis]
    copies = [
        pltpu.make_async_copy(source, target, sems.at[i])
        for i, (source, target) in enumerate(zip(sources + vectors_hbm, targets + vectors))
    ]
    for copy in copies:
        copy.start()

    wide_pos, col_pos, col_count = place[0], place[1], place[2]
    for i in range(near_count):
        near_table[i] = -1
    for i in range(len(far_places)):
        far_table[i] = -1

    def list_near(slot, carry):
        target = near_ids[0, slot]

        @pl.when(target >= 0)
        def _():
            row = near_slot(target // col_count, wide_pos)
            column = near_slot(target % col_count, col_pos)
            near_table[row * 3 + column] = slot

        return carry

    lax.fori_loop(0, near_ids.shape[1], list_near, 0)
    columns = 2 * REACH + 1

    def list_far(slot, carry):
        target = far_ids[0, slot]

        @pl.when(target >= 0)
        def _():
            row = far_row_slot(target // col_count, wide_pos, short)
            column = line_slot(target % col_count, col_pos)
            far_table[row * columns + column] = slot

        return carry

    lax.fori_loop(0, far_ids.shape[1], list_far, 0)

    done = 0

    def wait(count):
        nonlocal done
        for i in range(done, done + count):
            copies[i].wait()
        done += count

    wait(2)
    w_out[...] = mm_bf16(self_block[...], near[0][...])
    wait(near_count)
    for i in range(1, near_count):

        @pl.when(near_table[i] >= 0)
        def _():
            w_out[...] += mm_bf16(blocks[0, near_table[i]], near[i][...])

    wait(n_far + 2)
    rank = basis.shape[1]
    sums_out[:, :rank] = jnp.zeros((rank, sums_out.shape[0]), jnp.float32)
    for i, (array, part) in enumerate(far_places):

        @pl.when(far_table[i] >= 0)
        def _():
            piece = far[array][part * rank : (part + 1) * rank, :]
            sums_out[:, :rank] += mm_bf16(couplings[0, far_table[i]], piece)

    w_out[...] += mm_bf16(basis[...], sums_out[:, :rank].astype(jnp.bfloat16))
    wait(n_vectors)
    width = w_out.shape[1]
    for i in range(n_vectors):
        sums_out[:, i * width : (i + 1) * width] = mm(vectors[i][...], w_out[...], (0, 0))
    sums_out[:, n_vectors * width :] = mm(w_out[...], w_out[...], (0, 0))


def operate(zb, coef, basis, self_block, near_block, near_ids, couplings, far_ids, vectors):
    near, far = gather_windows(zb, coef)
    near_list = [near[row, column] for row in range(3) for column in range(3)]
    rows, width = zb.shape
    rank = basis.shape[1]
    arrays, places = [], []
    for key in sorted(far):
        array, part = far[key]
        known = [i for i, other in enumerate(arrays) if other is array]
        if not known:
            arrays.append(array)
        places.append((known[0] if known else len(arrays) - 1, part))
    place = jnp.stack(
        [lax.axis_index("wide"), lax.axis_index("col"), jnp.int32(lax.axis_size("col"))]
    ).astype(jnp.int32)
    big = near_list + arrays + [self_block, near_block, couplings, basis] + list(vectors)
    kernel = functools.partial(
        operator_kernel,
        near_count=len(near_list),
        far_places=tuple(places),
        n_far=len(arrays),
        n_vectors=len(vectors),
        short=short_wide(),
    )
    anywhere = pl.BlockSpec(memory_space=pl.ANY)
    return pl.pallas_call(
        kernel,
        out_shape=(
            jax.ShapeDtypeStruct((rows, width), jnp.float32),
            jax.ShapeDtypeStruct((width, (len(vectors) + 1) * width), jnp.float32),
        ),
        in_specs=[in_smem()] * 3 + [anywhere] * len(big),
        out_specs=(in_vmem(), in_vmem()),
        scratch_shapes=[pltpu.VMEM(a.shape, a.dtype) for a in big]
        + [
            pltpu.SMEM((len(near_list),), jnp.int32),
            pltpu.SMEM((len(places),), jnp.int32),
            pltpu.SemaphoreType.DMA((len(big),)),
        ],
        name="operator_kernel",
    )(near_ids, far_ids, place, *big)


def precondition(vb, top, bottom, starts, schwarz_inverse, basis):
    rows, width = vb.shape
    margin = top.shape[0]
    rank = basis.shape[1]
    before = along(bottom, "col", 1)
    after = along(top, "col", -1)
    centre = jnp.dot(
        schwarz_inverse[0, :, margin : margin + rows], vb, preferred_element_type=jnp.float32
    )
    low, high, mid = call(
        schwarz_kernel,
        [((margin, width), jnp.float32)] * 2 + [((rows, width), jnp.float32)],
        (),
        (schwarz_inverse, centre, before, after),
    )
    from_next = along(low, "col", -1)
    from_prev = along(high, "col", 1)
    return call(
        place_kernel,
        [((rows, width), jnp.float32), ((rows, width), jnp.bfloat16), ((rank, width), jnp.bfloat16)],
        (0,),
        (starts, mid, from_next, from_prev, basis),
        [pltpu.VMEM((rows + SUB, width), jnp.float32)],
    )


def on_device(
    rhs,
    basis,
    self_block,
    near_block,
    near_ids,
    couplings,
    far_ids,
    intersection_start,
    schwarz_inverse,
):
    rows, width = rhs.shape
    margin = (schwarz_inverse.shape[1] - rows) // 2
    square = ((width, width), jnp.float32)
    vector_shapes = [
        ((rows, width), jnp.float32),
        ((rows, width), jnp.bfloat16),
        ((margin, width), jnp.bfloat16),
        ((margin, width), jnp.bfloat16),
    ]
    work = [pltpu.VMEM((width, 2 * width), jnp.float32)]
    padded = [pltpu.VMEM((rows + SUB, width), jnp.float32)]
    fixed = (basis, self_block, near_block, near_ids, couplings, far_ids)

    gram0 = sum_everywhere(mm(rhs, rhs, (0, 0)), 2)
    v1, vb1, top1, bottom1, u0, c11 = call(
        first_kernel,
        vector_shapes + [square, square],
        (0,),
        (intersection_start, gram0, rhs),
        work + padded,
    )
    z1, zb1, coef1 = precondition(
        vb1, top1, bottom1, intersection_start, schwarz_inverse, basis
    )
    w1, part1 = operate(zb1, coef1, *fixed, (v1,))
    sums1 = sum_everywhere(part1, 3)
    v2, vb2, top2, bottom2, u1, inv1, gram1 = call(
        second_kernel,
        vector_shapes + [square, square, square],
        (0,),
        (intersection_start, sums1, c11, v1, w1),
        work + padded,
    )
    z2, zb2, coef2 = precondition(
        vb2, top2, bottom2, intersection_start, schwarz_inverse, basis
    )
    k_inv, t1, c12, c22 = call(
        third_kernel, [square] * 4, (), (sums1, c11, u0, inv1, gram1), work
    )
    w2, part2 = operate(zb2, coef2, *fixed, (v1, v2))
    sums2 = sum_everywhere(part2, 3)
    (solution_rows,) = call(
        last_kernel,
        [((rows, width), jnp.float32)],
        (),
        (sums2, sums1, c11, c12, c22, u0, u1, k_inv, t1, z1, z2),
        work,
    )
    return solution_rows


def solution(mesh):
    in_specs = (
        P(("wide", "col"), None),
        P(("wide", "col"), None),
        P(("wide", "col"), None),
        P(("wide", "col"), None, None, None),
        P(("wide", "col"), None),
        P(("wide", "col"), None, None, None),
        P(("wide", "col"), None),
        P(("wide", "col"), None),
        P(("wide", "col"), None, None),
    )
    out_specs = P(("wide", "col"), None)
    return jax.shard_map(
        on_device, mesh=mesh, in_specs=in_specs, out_specs=out_specs, check_vma=False
    )
```

```python
import functools

import jax
import jax.numpy as jnp
from jax import lax
from jax.experimental import pallas as pl
from jax.experimental.pallas import tpu as pltpu
from jax.sharding import PartitionSpec as P


REACH = 3
HIGHEST_PREC = lax.Precision.HIGHEST
SUB = 8
LANES = 128


def send(block, axis, route):
    return lax.ppermute(block, axis, route)


def along(block, axis, distance):
    count = lax.axis_size(axis)
    return send(
        block, axis, [(i, i + distance) for i in range(count) if 0 <= i + distance < count]
    )


def swap(block, axis, bit):
    return send(block, axis, [(i, i ^ bit) for i in range(lax.axis_size(axis))])


def outward(block, axis):
    count = lax.axis_size(axis)
    route = [(i, i + 1 if i % 2 else i - 1) for i in range(count)]
    return send(block, axis, [(s, t) for s, t in route if 0 <= t < count])


def relay(block, axis):
    count = lax.axis_size(axis)
    route = [(i, i - 2 if i % 2 else i + 2) for i in range(count)]
    return send(block, axis, [(s, t) for s, t in route if 0 <= t < count])


def is_even(axis):
    return lax.axis_index(axis) % 2 == 0


def split_sum(block, axis, bit):
    half = block.shape[0] // 2
    mine = (lax.axis_index(axis) // bit) % 2
    kept = lax.dynamic_slice_in_dim(block, mine * half, half, 0)
    given = lax.dynamic_slice_in_dim(block, (1 - mine) * half, half, 0)
    return kept + swap(given, axis, bit)


def join_halves(block, axis, bit):
    mine = (lax.axis_index(axis) // bit) % 2
    other = swap(block, axis, bit)
    return jnp.where(
        mine == 0,
        jnp.concatenate([block, other], axis=0),
        jnp.concatenate([other, block], axis=0),
    )


def is_power_of_two(count):
    return count & (count - 1) == 0


def sum_everywhere(block, splits):
    sizes = (lax.axis_size("wide"), lax.axis_size("col"))
    if not all(is_power_of_two(size) for size in sizes):
        return lax.psum(block, ("wide", "col"))
    stages = []
    for axis, size in zip(("wide", "col"), sizes):
        bit = 1
        while bit < size:
            stages.append((axis, bit))
            bit *= 2
    split_stages = stages[:splits]
    for axis, bit in split_stages:
        block = split_sum(block, axis, bit)
    for axis, bit in stages[splits:]:
        block = block + swap(block, axis, bit)
    for axis, bit in reversed(split_stages):
        block = join_halves(block, axis, bit)
    return block


def far_line(block, axis):
    rows = block.shape[0]
    pair = swap(block, axis, 1)
    both = jnp.concatenate([block, pair], axis=0)
    below = along(both, axis, 2)
    above = along(both, axis, -2)
    last = relay(jnp.where(is_even(axis), below[rows:], above[rows:]), axis)
    return [
        (block, 0),
        (pair, 0),
        (below, 0),
        (below, 1),
        (above, 0),
        (above, 1),
        (last, 0),
    ]


def line_slot(target, own):
    pair_step = target // 2 - own // 2
    other = (target + own) % 2
    return jnp.where(
        pair_step == 0,
        other,
        jnp.where(pair_step == -1, 2 + other, jnp.where(pair_step == 1, 4 + other, 6)),
    )


def near_slot(target, own):
    return jnp.where(target == own, 0, jnp.where(target // 2 == own // 2, 1, 2))


def short_wide():
    return lax.axis_size("wide") == REACH + 1


def far_row_slot(target, own, short):
    if short:
        same_pair = target // 2 == own // 2
        other = (target + own) % 2
        return jnp.where(same_pair, 0, 2) + other
    return line_slot(target, own)


def holds_outer(wide_pos):
    wide = lax.axis_size("wide")
    source = wide_pos - 1 if wide_pos % 2 == 0 else wide_pos + 1
    return 0 <= source < wide


def outer_send(block, step):
    cols = lax.axis_size("col")
    route = []
    for w in range(lax.axis_size("wide")):
        if not holds_outer(w):
            continue
        for c in range(cols):
            target = step(c)
            if 0 <= target < cols:
                route.append((w * cols + c, w * cols + target))
    return lax.ppermute(block, ("wide", "col"), route)


EARLY_COLUMNS = 2


def gather_windows(zb, coef):
    rank = coef.shape[0]
    xc = swap(coef, "col", 1)
    xn = swap(zb, "col", 1)
    yn = outward(zb, "wide")
    pair = jnp.concatenate([coef, xc], axis=0)
    zu = along(pair, "col", 2)
    zd = along(pair, "col", -2)
    xo = outer_send(yn, lambda c: c ^ 1)
    zn = relay(xn, "col")
    third = relay(jnp.where(is_even("col"), zu[rank:], zd[rank:]), "col")
    zo = outer_send(xo, lambda c: c - 2 if c % 2 else c + 2)
    near = {(0, 0): zb, (0, 1): xn, (0, 2): zn, (2, 0): yn, (2, 1): xo, (2, 2): zo}
    for col_slot in range(3):
        near[1, col_slot] = swap(near[0, col_slot], "wide", 1)
    own_line = [(coef, 0), (xc, 0), (zu, 0), (zu, 1), (zd, 0), (zd, 1), (third, 0)]
    far = {}
    if short_wide():
        yp = swap(pair, "wide", 2)
        quad = jnp.concatenate([zu, zd], axis=0)
        yq = swap(quad, "wide", 2)
        yt = swap(third, "wide", 2)
        ca = swap(jnp.concatenate([pair, yp], axis=0), "wide", 1)
        cq = swap(quad, "wide", 1)
        ct = swap(third, "wide", 1)
        cb = swap(jnp.concatenate([yq, yt], axis=0), "wide", 1)
        y_line = [(yp, 0), (yp, 1), (yq, 0), (yq, 1), (yq, 2), (yq, 3), (yt, 0)]
        c_line = [(ca, 0), (ca, 1), (cq, 0), (cq, 1), (cq, 2), (cq, 3), (ct, 0)]
        cy_line = [(ca, 2), (ca, 3), (cb, 0), (cb, 1), (cb, 2), (cb, 3), (cb, 4)]
        for wide_slot, line in enumerate((own_line, c_line, y_line, cy_line)):
            for col_slot, piece in enumerate(line):
                far[wide_slot, col_slot] = piece
    else:
        stacked = jnp.concatenate([coef, xc, zu, zd, third], axis=0)
        for wide_slot, (array, part) in enumerate(far_line(stacked, "wide")):
            for col_slot in range(2 * REACH + 1):
                far[wide_slot, col_slot] = (array, part * (2 * REACH + 1) + col_slot)
    return near, far


def mm(left, right, contract=(1, 0)):
    return lax.dot_general(
        left,
        right,
        (((contract[0],), (contract[1],)), ((), ())),
        precision=HIGHEST_PREC,
        preferred_element_type=jnp.float32,
    )


def mm_bf16(left, right, contract=(1, 0)):
    return lax.dot_general(
        left,
        right,
        (((contract[0],), (contract[1],)), ((), ())),
        preferred_element_type=jnp.float32,
    )


def row_across(tile, row):
    return jnp.broadcast_to(tile[row : row + 1, :], tile.shape)


def eliminate_strip(strip, pivots):
    rows = lax.broadcasted_iota(jnp.int32, (SUB, LANES), 0)
    columns = [
        jnp.broadcast_to(strip[:, pivots + j : pivots + j + 1], (SUB, LANES)) for j in range(SUB)
    ]
    tiles = [strip[:, t : t + LANES] for t in range(0, strip.shape[1], LANES)]
    for i in range(SUB):
        inverse_root = lax.rsqrt(row_across(columns[i], i))
        factor = jnp.where(rows > i, columns[i] * inverse_root, 0.0)
        for j in range(i + 1, SUB):
            columns[j] = columns[j] - factor * (row_across(columns[j], i) * inverse_root)
        for t in range(len(tiles)):
            scaled = row_across(tiles[t], i) * inverse_root
            tiles[t] = jnp.where(rows == i, scaled, tiles[t] - factor * scaled)
    return jnp.concatenate(tiles, axis=1)


def factorize(*works):
    size = works[0].shape[0]
    unit = (
        lax.broadcasted_iota(jnp.int32, (size, size), 0)
        == lax.broadcasted_iota(jnp.int32, (size, size), 1)
    ).astype(jnp.float32)
    for work in works:
        work[:, size:] = unit

    def panel(step, carry):
        first = pl.multiple_of(step * LANES, LANES)
        lanes = pl.ds(first, size + LANES)
        for top in range(0, LANES, SUB):
            here = pl.ds(first + top, SUB)
            strips = [eliminate_strip(work[here, lanes], top) for work in works]
            for work, strip in zip(works, strips):
                work[here, lanes] = strip
            turned = [strip[:, :LANES].T for strip in strips]
            for row in range(top + SUB, LANES, SUB):
                there = pl.ds(first + row, SUB)
                for work, strip, turn in zip(works, strips, turned):
                    block = turn[row : row + SUB, :]
                    rest = work[there, lanes]
                    for i in range(SUB):
                        rest = rest - jnp.broadcast_to(
                            block[:, i : i + 1], rest.shape
                        ) * jnp.broadcast_to(strip[i : i + 1, :], rest.shape)
                    work[there, lanes] = rest

        def below(part, inner):
            low = pl.multiple_of(part * LANES, LANES)
            for work in works:
                done = work[pl.ds(first, LANES), lanes]
                turned = work[pl.ds(first, LANES), pl.ds(low, LANES)]
                update = mm(turned, done, (0, 0))
                work[pl.ds(low, LANES), lanes] = work[pl.ds(low, LANES), lanes] - update
            return inner

        lax.fori_loop(step + 1, size // LANES, below, 0)
        return carry

    lax.fori_loop(0, size // LANES, panel, 0)


def upper(work):
    size = work.shape[0]
    keep = lax.broadcasted_iota(jnp.int32, (size, size), 1) >= lax.broadcasted_iota(
        jnp.int32, (size, size), 0
    )
    return jnp.where(keep, work[:, :size], 0.0)


def window_rows(padded, start, size):
    base = pl.multiple_of((start // SUB) * SUB, SUB)
    taken = padded[pl.ds(base, size + SUB), :]
    return pltpu.roll(taken, (size + SUB - start % SUB) % (size + SUB), 0)[:size]


def add_window(padded, start, addend):
    size = addend.shape[0]
    base = pl.multiple_of((start // SUB) * SUB, SUB)
    longer = jnp.concatenate([addend, jnp.zeros((SUB, addend.shape[1]), addend.dtype)], axis=0)
    span = pl.ds(base, size + SUB)
    padded[span, :] = padded[span, :] + pltpu.roll(longer, start % SUB, 0)


def write_vector(vector, starts, vb_out, top_out, bottom_out, padded):
    rows = vector.shape[0]
    vb_out[...] = vector.astype(jnp.bfloat16)
    padded[:rows, :] = vector
    padded[rows:, :] = jnp.zeros((SUB, vector.shape[1]), vector.dtype)
    margin = top_out.shape[0]
    top_out[...] = window_rows(padded, starts[0, 0], margin).astype(jnp.bfloat16)
    bottom_out[...] = window_rows(padded, starts[0, 1], margin).astype(jnp.bfloat16)


def first_kernel(starts, gram, rhs, v_out, vb_out, top_out, bottom_out, u_out, work, padded):
    size = gram.shape[0]
    work[:, :size] = gram[...]
    factorize(work)
    v = mm(rhs[...], work[:, size:], (1, 1))
    v_out[...] = v
    write_vector(v, starts, vb_out, top_out, bottom_out, padded)
    u_out[...] = upper(work)


def second_kernel(
    starts, sums, u0, v1, w, vb_out, top_out, bottom_out, k_inv_out, t1_out, work, other, padded
):
    size = u0.shape[0]
    h = sums[:, :size]
    work[:, :size] = sums[:, size:] - mm(h, h, (0, 0))
    other[:, :size] = sums[:, size:]
    factorize(work, other)
    rest = w[...] - mm(v1[...], h)
    v = mm(rest, work[:, size:], (1, 1))
    write_vector(v, starts, vb_out, top_out, bottom_out, padded)
    k_inverse = other[:, size:]
    k_inv_out[...] = k_inverse
    t1_out[...] = mm(k_inverse, mm(h, u0[...], (0, 0)))


def last_kernel(sums, u0, k_inv, t1, z1, z2, out, work):
    size = u0.shape[0]
    cross = mm(k_inv[...], sums[:, size : 2 * size])
    work[:, :size] = sums[:, 2 * size :] - mm(cross, cross, (0, 0))
    factorize(work)
    inverse = work[:, size:]
    t2 = mm(inverse, mm(sums[:, :size], u0[...], (0, 0)) - mm(cross, t1[...], (0, 0)))
    y2 = mm(inverse, t2, (0, 0))
    y1 = mm(k_inv[...], t1[...] - mm(cross, y2), (0, 0))
    out[...] = mm(z1[...], y1) + mm(z2[...], y2)


def edge_kernel(inverse, vb, before, after, low_out, high_out):
    margin = before.shape[0]
    rows = vb.shape[0]

    def of(rows_at):
        return (
            mm_bf16(inverse[0, rows_at, margin : margin + rows], vb[...])
            + mm_bf16(inverse[0, rows_at, :margin], before[...])
            + mm_bf16(inverse[0, rows_at, margin + rows :], after[...])
        )

    low_out[...] = of(slice(0, margin))
    high_out[...] = of(slice(margin + rows, None))


def middle_kernel(inverse, vb, before, after, mid_out):
    margin = before.shape[0]
    rows = vb.shape[0]
    at = slice(margin, margin + rows)
    mid_out[...] = (
        mm_bf16(inverse[0, at, margin : margin + rows], vb[...])
        + mm_bf16(inverse[0, at, :margin], before[...])
        + mm_bf16(inverse[0, at, margin + rows :], after[...])
    )


def place_kernel(starts, mid, from_next, from_prev, basis, z_out, zb_out, coef_out, padded):
    rows = mid.shape[0]
    padded[:rows, :] = mid[...]
    padded[rows:, :] = jnp.zeros((SUB, mid.shape[1]), jnp.float32)
    add_window(padded, starts[0, 1], from_next[...])
    add_window(padded, starts[0, 0], from_prev[...])
    z = padded[:rows, :]
    z_out[...] = z
    zb = z.astype(jnp.bfloat16)
    zb_out[...] = zb
    coef_out[...] = mm_bf16(basis[...], zb, (0, 0)).astype(jnp.bfloat16)


def in_vmem():
    return pl.BlockSpec(memory_space=pltpu.VMEM)


def in_smem():
    return pl.BlockSpec(memory_space=pltpu.SMEM)


def call(kernel, shapes, smem, args, scratch=()):
    specs = [in_smem() if i in smem else in_vmem() for i in range(len(args))]
    outs = tuple(jax.ShapeDtypeStruct(shape, dtype) for shape, dtype in shapes)
    return pl.pallas_call(
        kernel,
        out_shape=outs,
        in_specs=specs,
        out_specs=tuple(in_vmem() for _ in outs),
        scratch_shapes=list(scratch),
        compiler_params=pltpu.CompilerParams(vmem_limit_bytes=SMALL_VMEM),
    )(*args)


def field_kernel(*refs, n_near, near_from, far_places, n_far, far_from, n_vectors, late, short):
    it = iter(refs)
    near_at, far_at = next(it), next(it)
    near_hbm = [next(it) for _ in range(n_near)]
    far_hbm = [next(it) for _ in range(n_far)]
    blocks_hbm, couplings_hbm = next(it), next(it)
    fixed_hbm = [next(it) for _ in range(3 + n_vectors if late else 1)]
    w_out, sums_out = next(it), next(it)
    near, far, blocks, couplings = next(it), next(it), next(it), next(it)
    fixed = [next(it) for _ in fixed_hbm]
    near_table, near_sems, block_sems, far_sems, coupling_sems, fixed_sems = (
        next(it) for _ in range(6)
    )
    rows, width = w_out.shape
    rank = couplings.shape[1]
    near_columns = n_near // 3
    far_columns = len(far_places) // (REACH + 1 if short else 2 * REACH + 1)

    def near_copy(i):
        return pltpu.make_async_copy(
            near_hbm[i], near.at[pl.ds(i * rows, rows)], near_sems.at[i]
        )

    def far_copy(i):
        array, part = far_places[i]
        return pltpu.make_async_copy(
            far_hbm[array].at[pl.ds(part * rank, rank)],
            far.at[pl.ds(i * rank, rank)],
            far_sems.at[i],
        )

    def fixed_copy(i):
        return pltpu.make_async_copy(fixed_hbm[i], fixed[i], fixed_sems.at[i])

    def block_copy(slot, i):
        return pltpu.make_async_copy(blocks_hbm.at[0, slot], blocks.at[i], block_sems.at[i])

    def coupling_copy(slot):
        return pltpu.make_async_copy(
            couplings_hbm.at[0, slot], couplings.at[slot], coupling_sems.at[slot]
        )

    fixed_copy(0).start()
    for i in range(n_near):
        near_copy(i).start()
        near_table[i] = -1

    def list_near(slot, carry):
        row, column = near_at[0, slot], near_at[1, slot] - near_from

        @pl.when((row >= 0) & (column >= 0) & (column < near_columns))
        def _():
            i = row * near_columns + column
            near_table[i] = slot
            block_copy(slot, i).start()

        return carry

    lax.fori_loop(0, near_at.shape[1], list_near, 0)

    def far_position(slot):
        row, column = far_at[0, slot], far_at[1, slot] - far_from
        return (row >= 0) & (column >= 0) & (column < far_columns), row * far_columns + column

    def list_far(slot, carry):
        taken, _ = far_position(slot)

        @pl.when(taken)
        def _():
            coupling_copy(slot).start()

        return carry

    if far_places:
        for i in range(len(far_places)):
            far_copy(i).start()
        lax.fori_loop(0, far_at.shape[1], list_far, 0)
    for i in range(1, len(fixed)):
        fixed_copy(i).start()

    fixed_copy(0).wait()
    for i in range(n_near):
        near_copy(i).wait()
    if late:
        w_out[...] = fixed[0][...]
    else:
        w_out[...] = mm_bf16(fixed[0][...], near[:rows, :])

    def add_near(i, carry):
        slot = near_table[i]

        @pl.when(slot >= 0)
        def _():
            block_copy(slot, i).wait()
            at = pl.multiple_of(i * rows, rows)
            w_out[...] += mm_bf16(blocks[i], near[pl.ds(at, rows), :])

        return carry

    lax.fori_loop(0, n_near, add_near, 0)

    if late:
        fixed_copy(1).wait()
        sums_out[:, :width] = fixed[1][...]
    else:
        sums_out[...] = jnp.zeros((rank, width), jnp.float32)

    def add_far(slot, carry):
        taken, i = far_position(slot)

        @pl.when(taken)
        def _():
            coupling_copy(slot).wait()
            at = pl.multiple_of(i * rank, rank)
            sums_out[:, :width] += mm_bf16(couplings[slot], far[pl.ds(at, rank), :])

        return carry

    if far_places:
        for i in range(len(far_places)):
            far_copy(i).wait()
        lax.fori_loop(0, far_at.shape[1], add_far, 0)
    if late:
        fixed_copy(2).wait()
        w_out[...] += mm_bf16(fixed[2][...], sums_out[:, :width].astype(jnp.bfloat16))
        for i in range(n_vectors):
            fixed_copy(3 + i).wait()
            sums_out[:, i * width : (i + 1) * width] = mm(fixed[3 + i][...], w_out[...], (0, 0))
        sums_out[:, n_vectors * width :] = mm(w_out[...], w_out[...], (0, 0))


def field_call(ids, near, far, near_columns, far_columns, near_block, couplings, fixed, vectors, late):
    near_list = [near[r, c] for r in range(3) for c in near_columns]
    arrays, places = [], []
    for key in sorted(far):
        if key[1] not in far_columns:
            continue
        array, part = far[key]
        known = [i for i, other in enumerate(arrays) if other is array]
        if not known:
            arrays.append(array)
        places.append((known[0] if known else len(arrays) - 1, part))
    rows, width = near_list[0].shape
    rank = couplings.shape[2]
    fixed = list(fixed) + list(vectors)
    kernel = functools.partial(
        field_kernel,
        n_near=len(near_list),
        near_from=min(near_columns),
        far_places=tuple(places),
        n_far=len(arrays),
        far_from=min(far_columns) if far_columns else 0,
        n_vectors=len(vectors),
        late=late,
        short=short_wide(),
    )
    anywhere = pl.BlockSpec(memory_space=pl.ANY)
    args = near_list + arrays + [near_block, couplings] + fixed
    far_slots = max(len(places), 1)
    return pl.pallas_call(
        kernel,
        out_shape=(
            jax.ShapeDtypeStruct((rows, width), jnp.float32),
            jax.ShapeDtypeStruct((rank, (len(vectors) + 1) * width), jnp.float32),
        ),
        in_specs=[in_smem()] * 2 + [anywhere] * len(args),
        out_specs=(in_vmem(), in_vmem()),
        scratch_shapes=[
            pltpu.VMEM((len(near_list) * rows, width), jnp.bfloat16),
            pltpu.VMEM((far_slots * rank, width), jnp.bfloat16),
            pltpu.VMEM((len(near_list), rows, rows), near_block.dtype),
            pltpu.VMEM(couplings.shape[1:], couplings.dtype),
        ]
        + [pltpu.VMEM(a.shape, a.dtype) for a in fixed]
        + [
            pltpu.SMEM((len(near_list),), jnp.int32),
            pltpu.SemaphoreType.DMA((len(near_list),)),
            pltpu.SemaphoreType.DMA((len(near_list),)),
            pltpu.SemaphoreType.DMA((far_slots,)),
            pltpu.SemaphoreType.DMA((couplings.shape[1],)),
            pltpu.SemaphoreType.DMA((len(fixed),)),
        ],
        compiler_params=pltpu.CompilerParams(vmem_limit_bytes=FIELD_VMEM),
        name="late_kernel" if late else "early_kernel",
    )(*ids, *args)


FIELD_VMEM = 40 * 1024 * 1024
SMALL_VMEM = 16 * 1024 * 1024


def slot_places(ids, row_slot, column_slot):
    cols = lax.axis_size("col")
    targets = jnp.maximum(ids[0], 0)
    rows = row_slot(targets // cols, lax.axis_index("wide"))
    columns = column_slot(targets % cols, lax.axis_index("col"))
    return jnp.stack([jnp.where(ids[0] >= 0, rows, -1), columns]).astype(jnp.int32)


def operate(zb, coef, basis, self_block, near_block, ids, couplings, vectors):
    near, far = gather_windows(zb, coef)
    every = list(range(2 * REACH + 1))
    early = every[:EARLY_COLUMNS] if short_wide() else []
    w, far_sum = field_call(
        ids, near, far, (0, 1), early, near_block, couplings, (self_block,), (), False
    )
    return field_call(
        ids,
        near,
        far,
        (2,),
        every[len(early) :],
        near_block,
        couplings,
        (w, far_sum, basis),
        vectors,
        True,
    )


def precondition(vb, top, bottom, starts, schwarz_inverse, basis):
    rows, width = vb.shape
    margin = top.shape[0]
    rank = basis.shape[1]
    before = along(bottom, "col", 1)
    after = along(top, "col", -1)
    args = (schwarz_inverse, vb, before, after)
    edge = ((margin, width), jnp.float32)
    low, high = call(edge_kernel, [edge, edge], (), args)
    from_next = along(low, "col", -1)
    from_prev = along(high, "col", 1)
    (mid,) = call(middle_kernel, [((rows, width), jnp.float32)], (), args)
    return call(
        place_kernel,
        [((rows, width), jnp.float32), ((rows, width), jnp.bfloat16), ((rank, width), jnp.bfloat16)],
        (0,),
        (starts, mid, from_next, from_prev, basis),
        [pltpu.VMEM((rows + SUB, width), jnp.float32)],
    )


def on_device(
    rhs,
    basis,
    self_block,
    near_block,
    near_ids,
    couplings,
    far_ids,
    intersection_start,
    schwarz_inverse,
):
    rows, width = rhs.shape
    margin = (schwarz_inverse.shape[1] - rows) // 2
    square = ((width, width), jnp.float32)
    whole = ((rows, width), jnp.float32)
    sent = [
        ((rows, width), jnp.bfloat16),
        ((margin, width), jnp.bfloat16),
        ((margin, width), jnp.bfloat16),
    ]
    work = [pltpu.VMEM((width, 2 * width), jnp.float32)]
    padded = [pltpu.VMEM((rows + SUB, width), jnp.float32)]
    row_slot = functools.partial(far_row_slot, short=short_wide())
    ids = (
        slot_places(near_ids, near_slot, near_slot),
        slot_places(far_ids, row_slot, line_slot),
    )
    fixed = (basis, self_block, near_block, ids, couplings)

    gram0 = sum_everywhere(mm(rhs, rhs, (0, 0)), 2)
    v1, vb1, top1, bottom1, u0 = call(
        first_kernel,
        [whole] + sent + [square],
        (0,),
        (intersection_start, gram0, rhs),
        work + padded,
    )
    z1, zb1, coef1 = precondition(vb1, top1, bottom1, intersection_start, schwarz_inverse, basis)
    w1, part1 = operate(zb1, coef1, *fixed, (v1,))
    sums1 = sum_everywhere(part1, 3)
    vb2, top2, bottom2, k_inv, t1 = call(
        second_kernel,
        sent + [square, square],
        (0,),
        (intersection_start, sums1, u0, v1, w1),
        work + work + padded,
    )
    z2, zb2, coef2 = precondition(vb2, top2, bottom2, intersection_start, schwarz_inverse, basis)
    _, part2 = operate(zb2, coef2, *fixed, (v1, w1))
    sums2 = sum_everywhere(part2, 3)
    (solution_rows,) = call(
        last_kernel, [whole], (), (sums2, u0, k_inv, t1, z1, z2), work
    )
    return solution_rows


def solution(mesh):
    in_specs = (
        P(("wide", "col"), None),
        P(("wide", "col"), None),
        P(("wide", "col"), None),
        P(("wide", "col"), None, None, None),
        P(("wide", "col"), None),
        P(("wide", "col"), None, None, None),
        P(("wide", "col"), None),
        P(("wide", "col"), None),
        P(("wide", "col"), None, None),
    )
    out_specs = P(("wide", "col"), None)
    return jax.shard_map(
        on_device, mesh=mesh, in_specs=in_specs, out_specs=out_specs, check_vma=False
    )
```

```python
import functools

import jax
import jax.numpy as jnp
from jax import lax
from jax.experimental import pallas as pl
from jax.experimental.pallas import tpu as pltpu
from jax.sharding import PartitionSpec as P


REACH = 3
HIGHEST_PREC = lax.Precision.HIGHEST
SUB = 8
LANES = 128


def send(block, axis, route):
    return lax.ppermute(block, axis, route)


def along(block, axis, distance):
    count = lax.axis_size(axis)
    return send(
        block, axis, [(i, i + distance) for i in range(count) if 0 <= i + distance < count]
    )


def swap(block, axis, bit):
    return send(block, axis, [(i, i ^ bit) for i in range(lax.axis_size(axis))])


def outward(block, axis):
    count = lax.axis_size(axis)
    route = [(i, i + 1 if i % 2 else i - 1) for i in range(count)]
    return send(block, axis, [(s, t) for s, t in route if 0 <= t < count])


def relay(block, axis):
    count = lax.axis_size(axis)
    route = [(i, i - 2 if i % 2 else i + 2) for i in range(count)]
    return send(block, axis, [(s, t) for s, t in route if 0 <= t < count])


def is_even(axis):
    return lax.axis_index(axis) % 2 == 0


def join_halves(block, axis, bit):
    mine = (lax.axis_index(axis) // bit) % 2
    other = swap(block, axis, bit)
    return jnp.where(
        mine == 0,
        jnp.concatenate([block, other], axis=0),
        jnp.concatenate([other, block], axis=0),
    )


def sum_stages():
    stages = []
    for axis in ("wide", "col"):
        size = lax.axis_size(axis)
        if size & (size - 1):
            raise ValueError("axis size")
        stages += [(axis, 1 << k) for k in range(size.bit_length() - 1)]
    return stages


SPLITS = 3


def split_bits():
    sides = [(lax.axis_index(axis) // bit) % 2 for axis, bit in sum_stages()[:SPLITS]]
    return jnp.stack(sides).astype(jnp.int32)


def halves(total, side):
    half = total.shape[0] // 2
    kept = pl.multiple_of(side * half, SUB)
    given = pl.multiple_of((1 - side) * half, SUB)
    return total[pl.ds(kept, half), :], total[pl.ds(given, half), :]


def split_kernel(bits, kept, received, kept_out, given_out, total, *, stage):
    total[...] = kept[...] + received[...]
    kept_out[...], given_out[...] = halves(total, bits[stage])


def sum_everywhere(kept, given, bits, splits):
    stages = sum_stages()
    for stage, (axis, bit) in enumerate(stages[:splits]):
        received = swap(given, axis, bit)
        if stage + 1 < splits:
            rows, width = kept.shape
            kept, given = call(
                functools.partial(split_kernel, stage=stage + 1),
                [((rows // 2, width), jnp.float32)] * 2,
                (0,),
                (bits, kept, received),
                [pltpu.VMEM((rows, width), jnp.float32)],
            )
        else:
            block = kept + received
    for axis, bit in stages[splits:]:
        block = block + swap(block, axis, bit)
    for axis, bit in reversed(stages[:splits]):
        block = join_halves(block, axis, bit)
    return block


def far_line(block, axis):
    rows = block.shape[0]
    pair = swap(block, axis, 1)
    both = jnp.concatenate([block, pair], axis=0)
    below = along(both, axis, 2)
    above = along(both, axis, -2)
    last = relay(jnp.where(is_even(axis), below[rows:], above[rows:]), axis)
    return [
        (block, 0),
        (pair, 0),
        (below, 0),
        (below, 1),
        (above, 0),
        (above, 1),
        (last, 0),
    ]


def line_slot(target, own):
    pair_step = target // 2 - own // 2
    other = (target + own) % 2
    return jnp.where(
        pair_step == 0,
        other,
        jnp.where(pair_step == -1, 2 + other, jnp.where(pair_step == 1, 4 + other, 6)),
    )


def near_slot(target, own):
    return jnp.where(target == own, 0, jnp.where(target // 2 == own // 2, 1, 2))


def short_wide():
    return lax.axis_size("wide") == REACH + 1


def far_row_slot(target, own, short):
    if short:
        same_pair = target // 2 == own // 2
        other = (target + own) % 2
        return jnp.where(same_pair, 0, 2) + other
    return line_slot(target, own)


def holds_outer(wide_pos):
    wide = lax.axis_size("wide")
    source = wide_pos - 1 if wide_pos % 2 == 0 else wide_pos + 1
    return 0 <= source < wide


def outer_send(block, step):
    cols = lax.axis_size("col")
    route = []
    for w in range(lax.axis_size("wide")):
        if not holds_outer(w):
            continue
        for c in range(cols):
            target = step(c)
            if 0 <= target < cols:
                route.append((w * cols + c, w * cols + target))
    return lax.ppermute(block, ("wide", "col"), route)


def gather_windows(zb, coef):
    rank = coef.shape[0]
    xc = swap(coef, "col", 1)
    xn = swap(zb, "col", 1)
    yn = outward(zb, "wide")
    pair = jnp.concatenate([coef, xc], axis=0)
    zu = along(pair, "col", 2)
    zd = along(pair, "col", -2)
    xo = outer_send(yn, lambda c: c ^ 1)
    zn = relay(xn, "col")
    third = relay(jnp.where(is_even("col"), zu[rank:], zd[rank:]), "col")
    zo = outer_send(xo, lambda c: c - 2 if c % 2 else c + 2)
    near = {(0, 0): zb, (0, 1): xn, (0, 2): zn, (2, 0): yn, (2, 1): xo, (2, 2): zo}
    for col_slot in range(3):
        near[1, col_slot] = swap(near[0, col_slot], "wide", 1)
    own_line = [(coef, 0), (xc, 0), (zu, 0), (zu, 1), (zd, 0), (zd, 1), (third, 0)]
    far = {}
    if short_wide():
        yp = swap(pair, "wide", 2)
        quad = jnp.concatenate([zu, zd], axis=0)
        yq = swap(quad, "wide", 2)
        yt = swap(third, "wide", 2)
        ca = swap(jnp.concatenate([pair, yp], axis=0), "wide", 1)
        cq = swap(quad, "wide", 1)
        ct = swap(third, "wide", 1)
        cb = swap(jnp.concatenate([yq, yt], axis=0), "wide", 1)
        y_line = [(yp, 0), (yp, 1), (yq, 0), (yq, 1), (yq, 2), (yq, 3), (yt, 0)]
        c_line = [(ca, 0), (ca, 1), (cq, 0), (cq, 1), (cq, 2), (cq, 3), (ct, 0)]
        cy_line = [(ca, 2), (ca, 3), (cb, 0), (cb, 1), (cb, 2), (cb, 3), (cb, 4)]
        for wide_slot, line in enumerate((own_line, c_line, y_line, cy_line)):
            for col_slot, piece in enumerate(line):
                far[wide_slot, col_slot] = piece
    else:
        stacked = jnp.concatenate([coef, xc, zu, zd, third], axis=0)
        for wide_slot, (array, part) in enumerate(far_line(stacked, "wide")):
            for col_slot in range(2 * REACH + 1):
                far[wide_slot, col_slot] = (array, part * (2 * REACH + 1) + col_slot)
    return near, far


def mm(left, right, contract=(1, 0)):
    return lax.dot_general(
        left,
        right,
        (((contract[0],), (contract[1],)), ((), ())),
        precision=HIGHEST_PREC,
        preferred_element_type=jnp.float32,
    )


def mm_bf16(left, right, contract=(1, 0)):
    return lax.dot_general(
        left,
        right,
        (((contract[0],), (contract[1],)), ((), ())),
        preferred_element_type=jnp.float32,
    )


def row_across(tile, row):
    return jnp.broadcast_to(tile[row : row + 1, :], tile.shape)


def eliminate_strip(strip, pivots):
    rows = lax.broadcasted_iota(jnp.int32, (SUB, LANES), 0)
    columns = [
        jnp.broadcast_to(strip[:, pivots + j : pivots + j + 1], (SUB, LANES)) for j in range(SUB)
    ]
    tiles = [strip[:, t : t + LANES] for t in range(0, strip.shape[1], LANES)]
    for i in range(SUB):
        pivot = row_across(columns[i], i)
        products = [columns[i] * row_across(columns[j], i) for j in range(i + 1, SUB)]
        inverse_root = lax.rsqrt(pivot)
        inverse = inverse_root * inverse_root
        for j in range(i + 1, SUB):
            columns[j] = columns[j] - products[j - i - 1] * inverse
        factor = jnp.where(rows > i, columns[i] * inverse_root, 0.0)
        for t in range(len(tiles)):
            scaled = row_across(tiles[t], i) * inverse_root
            tiles[t] = jnp.where(rows == i, scaled, tiles[t] - factor * scaled)
    return jnp.concatenate(tiles, axis=1)


def factorize(*works):
    size = works[0].shape[0]
    unit = (
        lax.broadcasted_iota(jnp.int32, (size, size), 0)
        == lax.broadcasted_iota(jnp.int32, (size, size), 1)
    ).astype(jnp.float32)
    for work in works:
        work[:, size:] = unit

    def panel(step, carry):
        first = pl.multiple_of(step * LANES, LANES)
        lanes = pl.ds(first, size + LANES)
        count = LANES // SUB
        panels = [[w[pl.ds(first + k * SUB, SUB), lanes] for k in range(count)] for w in works]
        for k in range(count):
            for work, strips in zip(works, panels):
                strips[k] = eliminate_strip(strips[k], k * SUB)
                work[pl.ds(first + k * SUB, SUB), lanes] = strips[k]
            turned = [strips[k][:, :LANES].T for strips in panels]
            for q in range(k + 1, count):
                for strips, turn in zip(panels, turned):
                    block = turn[q * SUB : (q + 1) * SUB, :]
                    rest = strips[q]
                    for i in range(SUB):
                        rest = rest - jnp.broadcast_to(
                            block[:, i : i + 1], rest.shape
                        ) * jnp.broadcast_to(strips[k][i : i + 1, :], rest.shape)
                    strips[q] = rest

        def below(part, inner):
            low = pl.multiple_of(part * LANES, LANES)
            for work in works:
                done = work[pl.ds(first, LANES), lanes]
                turned = work[pl.ds(first, LANES), pl.ds(low, LANES)]
                update = mm(turned, done, (0, 0))
                work[pl.ds(low, LANES), lanes] = work[pl.ds(low, LANES), lanes] - update
            return inner

        lax.fori_loop(step + 1, size // LANES, below, 0)
        return carry

    lax.fori_loop(0, size // LANES, panel, 0)


def upper(work):
    size = work.shape[0]
    keep = lax.broadcasted_iota(jnp.int32, (size, size), 1) >= lax.broadcasted_iota(
        jnp.int32, (size, size), 0
    )
    return jnp.where(keep, work[:, :size], 0.0)


def window_rows(padded, start, size):
    base = pl.multiple_of((start // SUB) * SUB, SUB)
    taken = padded[pl.ds(base, size + SUB), :]
    return pltpu.roll(taken, (size + SUB - start % SUB) % (size + SUB), 0)[:size]


def add_window(padded, start, addend):
    size = addend.shape[0]
    base = pl.multiple_of((start // SUB) * SUB, SUB)
    longer = jnp.concatenate([addend, jnp.zeros((SUB, addend.shape[1]), addend.dtype)], axis=0)
    span = pl.ds(base, size + SUB)
    padded[span, :] = padded[span, :] + pltpu.roll(longer, start % SUB, 0)


def write_vector(vector, starts, vb_out, top_out, bottom_out, padded):
    rows = vector.shape[0]
    vb_out[...] = vector.astype(jnp.bfloat16)
    padded[:rows, :] = vector
    padded[rows:, :] = jnp.zeros((SUB, vector.shape[1]), vector.dtype)
    margin = top_out.shape[0]
    top_out[...] = window_rows(padded, starts[0, 0], margin).astype(jnp.bfloat16)
    bottom_out[...] = window_rows(padded, starts[0, 1], margin).astype(jnp.bfloat16)


def gram_kernel(bits, rhs, kept_out, given_out, total):
    total[...] = mm(rhs[...], rhs[...], (0, 0))
    kept_out[...], given_out[...] = halves(total, bits[0])


def first_kernel(starts, gram, rhs, v_out, vb_out, top_out, bottom_out, u_out, work, padded):
    size = gram.shape[0]
    work[:, :size] = gram[...]
    factorize(work)
    v = mm(rhs[...], work[:, size:], (1, 1))
    v_out[...] = v
    write_vector(v, starts, vb_out, top_out, bottom_out, padded)
    u_out[...] = upper(work)


def second_kernel(
    starts, sums, u0, v1, w, vb_out, top_out, bottom_out, k_inv_out, t1_out, work, other, padded
):
    size = u0.shape[0]
    h = sums[:, :size]
    work[:, :size] = sums[:, size:] - mm(h, h, (0, 0))
    other[:, :size] = sums[:, size:]
    factorize(work, other)
    rest = w[...] - mm(v1[...], h)
    v = mm(rest, work[:, size:], (1, 1))
    write_vector(v, starts, vb_out, top_out, bottom_out, padded)
    k_inverse = other[:, size:]
    k_inv_out[...] = k_inverse
    t1_out[...] = mm(k_inverse, mm(h, u0[...], (0, 0)))


def last_kernel(sums, u0, k_inv, t1, z1, z2, out, work, weights):
    size = u0.shape[0]
    cross = mm(k_inv[...], sums[:, size : 2 * size])
    work[:, :size] = sums[:, 2 * size :] - mm(cross, cross, (0, 0))
    factorize(work)
    inverse = work[:, size:]
    t2 = mm(inverse, mm(sums[:, :size], u0[...], (0, 0)) - mm(cross, t1[...], (0, 0)))
    y2 = mm(inverse, t2, (0, 0))
    y1 = mm(k_inv[...], t1[...] - mm(cross, y2), (0, 0))
    weights[:size, :] = y1
    weights[size:, :] = y2

    def rows_out(part, carry):
        at = pl.ds(pl.multiple_of(part * size, size), size)
        out[at, :] = mm(z1[at, :], weights[:size, :]) + mm(z2[at, :], weights[size:, :])
        return carry

    lax.fori_loop(0, out.shape[0] // size, rows_out, 0)


def edge_kernel(inverse, vb, before, after, low_out, high_out):
    margin = before.shape[0]
    rows = vb.shape[0]

    def of(rows_at):
        return (
            mm_bf16(inverse[0, rows_at, margin : margin + rows], vb[...])
            + mm_bf16(inverse[0, rows_at, :margin], before[...])
            + mm_bf16(inverse[0, rows_at, margin + rows :], after[...])
        )

    low_out[...] = of(slice(0, margin))
    high_out[...] = of(slice(margin + rows, None))


def middle_kernel(inverse, vb, before, after, mid_out):
    margin = before.shape[0]
    rows = vb.shape[0]
    at = slice(margin, margin + rows)
    mid_out[...] = (
        mm_bf16(inverse[0, at, margin : margin + rows], vb[...])
        + mm_bf16(inverse[0, at, :margin], before[...])
        + mm_bf16(inverse[0, at, margin + rows :], after[...])
    )


def place_kernel(starts, mid, from_next, from_prev, basis, z_out, zb_out, coef_out, padded):
    rows = mid.shape[0]
    padded[:rows, :] = mid[...]
    padded[rows:, :] = jnp.zeros((SUB, mid.shape[1]), jnp.float32)
    add_window(padded, starts[0, 1], from_next[...])
    add_window(padded, starts[0, 0], from_prev[...])
    z = padded[:rows, :]
    z_out[...] = z
    zb = z.astype(jnp.bfloat16)
    zb_out[...] = zb
    coef_out[...] = mm_bf16(basis[...], zb, (0, 0)).astype(jnp.bfloat16)


def in_vmem():
    return pl.BlockSpec(memory_space=pltpu.VMEM)


def in_smem():
    return pl.BlockSpec(memory_space=pltpu.SMEM)


def call(kernel, shapes, smem, args, scratch=(), vmem=None, anywhere=()):
    specs = [in_smem() if i in smem else in_vmem() for i in range(len(args))]
    args = list(args)
    for i in anywhere:
        specs[i] = pl.BlockSpec(memory_space=pltpu.HBM)
        args[i] = pltpu.with_memory_space_constraint(args[i], pltpu.HBM)
    outs = tuple(jax.ShapeDtypeStruct(shape, dtype) for shape, dtype in shapes)
    return pl.pallas_call(
        kernel,
        out_shape=outs,
        in_specs=specs,
        out_specs=tuple(in_vmem() for _ in outs),
        scratch_shapes=list(scratch),
        compiler_params=pltpu.CompilerParams(vmem_limit_bytes=vmem or SMALL_VMEM),
    )(*args)


NEAR_SIDE = 3
FAR_GROUP = 4
FIELD_VMEM = 28 * 1024 * 1024
SMALL_VMEM = 16 * 1024 * 1024


def block_copy(near_at, first, i, blocks_hbm, blocks, sems):
    slot = jnp.maximum(near_at[first + i], 0)
    return pltpu.make_async_copy(blocks_hbm.at[0, slot], blocks.at[i], sems.at[i])


def add_near(near_at, first, stack, blocks_hbm, blocks, sems, w_out):
    rows = w_out.shape[0]

    def add(i, carry):
        block_copy(near_at, first, i, blocks_hbm, blocks, sems).wait()

        @pl.when(near_at[first + i] >= 0)
        def _():
            at = pl.multiple_of(i * rows, rows)
            w_out[...] += mm_bf16(blocks[i], stack[pl.ds(at, rows), :])

        return carry

    lax.fori_loop(0, blocks.shape[0], add, 0)


NEAR_ORDER = (0, 3, 6, 1, 4, 7, 2, 5, 8)
EARLY = 6


def stack_pieces(pieces, stack):
    rows = pieces[0].shape[0]
    for i, piece in enumerate(pieces):
        stack[i * rows : (i + 1) * rows, :] = piece[...]


def early_kernel(near_at, *refs):
    *pieces, self_block, blocks_hbm, w_out, stack, blocks, sems = refs
    for i in range(EARLY - 1):
        block_copy(near_at, 1, i, blocks_hbm, blocks, sems).start()
    w_out[...] = mm_bf16(self_block[...], pieces[0][...])
    stack_pieces(pieces[1:], stack)
    add_near(near_at, 1, stack, blocks_hbm, blocks, sems, w_out)


def late_kernel(near_at, far_at, bits, *refs, far_places, n_far, n_vectors):
    it = iter(refs)
    pieces = [next(it) for _ in range(NEAR_SIDE)]
    far_arrays = [next(it) for _ in range(n_far)]
    w_in, blocks_hbm, couplings, basis = (next(it) for _ in range(4))
    vectors = [next(it) for _ in range(n_vectors)]
    w_out, kept_out, given_out, far, total, stack, blocks, sems = it
    for i in range(NEAR_SIDE):
        block_copy(near_at, EARLY, i, blocks_hbm, blocks, sems).start()
    stack_pieces(pieces, stack)
    rank = basis.shape[1]
    width = w_out.shape[1]
    for i, (array, part) in enumerate(far_places):
        far[i * rank : (i + 1) * rank, :] = far_arrays[array][part * rank : (part + 1) * rank, :]
    last = len(far_places) * rank
    far[last:, :] = jnp.zeros((rank, width), far.dtype)
    total[:, :width] = jnp.zeros((rank, width), jnp.float32)
    slots = couplings.shape[1]

    def add_group(group, carry):
        def product(slot):
            at = pl.multiple_of(far_at[slot] * rank, rank)
            return mm_bf16(couplings[0, slot], far[pl.ds(at, rank), :])

        first = group * FAR_GROUP
        added = product(first)
        for k in range(1, FAR_GROUP):
            added = added + product(first + k)
        total[:, :width] += added
        return carry

    lax.fori_loop(0, far_at[slots], add_group, 0)
    w_out[...] = w_in[...] + mm_bf16(basis[...], total[:, :width].astype(jnp.bfloat16))
    add_near(near_at, EARLY, stack, blocks_hbm, blocks, sems, w_out)
    total[...] = jnp.zeros(total.shape, jnp.float32)
    rows = w_out.shape[0]

    def add_grams(part, carry):
        at = pl.ds(pl.multiple_of(part * width, width), width)
        for i, vector in enumerate(vectors + [w_out]):
            total[:, i * width : (i + 1) * width] += mm(vector[at, :], w_out[at, :], (0, 0))
        return carry

    lax.fori_loop(0, rows // width, add_grams, 0)
    kept_out[...], given_out[...] = halves(total, bits[0])


def window_tables(near_ids, far_ids, far_slots):
    cols = lax.axis_size("col")
    wide_pos, col_pos = lax.axis_index("wide"), lax.axis_index("col")
    ids = near_ids[0]
    safe = jnp.maximum(ids, 0)
    at = near_slot(safe // cols, wide_pos) * NEAR_SIDE + near_slot(safe % cols, col_pos)
    positions = jnp.array(NEAR_ORDER)
    hit = (at[None, :] == positions[:, None]) & (ids >= 0)[None, :]
    near_at = jnp.max(jnp.where(hit, jnp.arange(ids.shape[0])[None, :], -1), axis=1)
    ids = far_ids[0]
    safe = jnp.maximum(ids, 0)
    row = far_row_slot(safe // cols, wide_pos, short_wide())
    at = row * (2 * REACH + 1) + line_slot(safe % cols, col_pos)
    live = ids >= 0
    groups = (jnp.sum(live.astype(jnp.int32)) + FAR_GROUP - 1) // FAR_GROUP
    far_at = jnp.concatenate([jnp.where(live, at, far_slots), groups[None]])
    return near_at.astype(jnp.int32), far_at.astype(jnp.int32)


def far_slot_count():
    rows = REACH + 1 if short_wide() else 2 * REACH + 1
    return rows * (2 * REACH + 1)


def operate(zb, coef, basis, self_block, near_block, tables, couplings, bits, vectors):
    near, far = gather_windows(zb, coef)
    near_at, far_at = tables
    rows, width = zb.shape
    rank = basis.shape[1]
    whole = ((rows, width), jnp.float32)
    pieces = [near[divmod(position, NEAR_SIDE)] for position in NEAR_ORDER]
    early = pieces[:EARLY]
    (w,) = call(
        early_kernel,
        [whole],
        (0,),
        (near_at, *early, self_block, near_block),
        [
            pltpu.VMEM(((EARLY - 1) * rows, width), jnp.bfloat16),
            pltpu.VMEM((EARLY - 1, rows, rows), near_block.dtype),
            pltpu.SemaphoreType.DMA((EARLY - 1,)),
        ],
        vmem=FIELD_VMEM,
        anywhere=(len(early) + 2,),
    )
    arrays, places = [], []
    for key in sorted(far):
        array, part = far[key]
        known = [i for i, other in enumerate(arrays) if other is array]
        if not known:
            arrays.append(array)
        places.append((known[0] if known else len(arrays) - 1, part))
    sums_width = (len(vectors) + 1) * width
    half = ((width // 2, sums_width), jnp.float32)
    return call(
        functools.partial(
            late_kernel,
            far_places=tuple(places),
            n_far=len(arrays),
            n_vectors=len(vectors),
        ),
        [whole, half, half],
        (0, 1, 2),
        (
            near_at,
            far_at,
            bits,
            *pieces[len(early) :],
            *arrays,
            w,
            near_block,
            couplings,
            basis,
            *vectors,
        ),
        [
            pltpu.VMEM(((len(places) + 1) * rank, width), jnp.bfloat16),
            pltpu.VMEM((width, sums_width), jnp.float32),
            pltpu.VMEM((NEAR_SIDE * rows, width), jnp.bfloat16),
            pltpu.VMEM((NEAR_SIDE, rows, rows), near_block.dtype),
            pltpu.SemaphoreType.DMA((NEAR_SIDE,)),
        ],
        vmem=FIELD_VMEM,
        anywhere=(3 + NEAR_SIDE + len(arrays) + 1,),
    )


def precondition(vb, top, bottom, starts, schwarz_inverse, basis):
    rows, width = vb.shape
    margin = top.shape[0]
    rank = basis.shape[1]
    before = along(bottom, "col", 1)
    after = along(top, "col", -1)
    args = (schwarz_inverse, vb, before, after)
    edge = ((margin, width), jnp.float32)
    low, high = call(edge_kernel, [edge, edge], (), args)
    from_next = along(low, "col", -1)
    from_prev = along(high, "col", 1)
    (mid,) = call(middle_kernel, [((rows, width), jnp.float32)], (), args)
    return call(
        place_kernel,
        [((rows, width), jnp.float32), ((rows, width), jnp.bfloat16), ((rank, width), jnp.bfloat16)],
        (0,),
        (starts, mid, from_next, from_prev, basis),
        [pltpu.VMEM((rows + SUB, width), jnp.float32)],
    )


def on_device(
    rhs,
    basis,
    self_block,
    near_block,
    near_ids,
    couplings,
    far_ids,
    intersection_start,
    schwarz_inverse,
):
    rows, width = rhs.shape
    margin = (schwarz_inverse.shape[1] - rows) // 2
    square = ((width, width), jnp.float32)
    whole = ((rows, width), jnp.float32)
    sent = [
        ((rows, width), jnp.bfloat16),
        ((margin, width), jnp.bfloat16),
        ((margin, width), jnp.bfloat16),
    ]
    work = [pltpu.VMEM((width, 2 * width), jnp.float32)]
    padded = [pltpu.VMEM((rows + SUB, width), jnp.float32)]
    bits = split_bits()
    tables = window_tables(near_ids, far_ids, far_slot_count())
    fixed = (basis, self_block, near_block, tables, couplings, bits)

    half = ((width // 2, width), jnp.float32)
    kept0, given0 = call(
        gram_kernel, [half, half], (0,), (bits, rhs), [pltpu.VMEM((width, width), jnp.float32)]
    )
    gram0 = sum_everywhere(kept0, given0, bits, 2)
    v1, vb1, top1, bottom1, u0 = call(
        first_kernel,
        [whole] + sent + [square],
        (0,),
        (intersection_start, gram0, rhs),
        work + padded,
    )
    z1, zb1, coef1 = precondition(vb1, top1, bottom1, intersection_start, schwarz_inverse, basis)
    w1, kept1, given1 = operate(zb1, coef1, *fixed, (v1,))
    sums1 = sum_everywhere(kept1, given1, bits, SPLITS)
    vb2, top2, bottom2, k_inv, t1 = call(
        second_kernel,
        sent + [square, square],
        (0,),
        (intersection_start, sums1, u0, v1, w1),
        work + work + padded,
    )
    z2, zb2, coef2 = precondition(vb2, top2, bottom2, intersection_start, schwarz_inverse, basis)
    _, kept2, given2 = operate(zb2, coef2, *fixed, (v1, w1))
    sums2 = sum_everywhere(kept2, given2, bits, SPLITS)
    (solution_rows,) = call(
        last_kernel,
        [whole],
        (),
        (sums2, u0, k_inv, t1, z1, z2),
        work + [pltpu.VMEM((2 * width, width), jnp.float32)],
    )
    return solution_rows


def solution(mesh):
    in_specs = (
        P(("wide", "col"), None),
        P(("wide", "col"), None),
        P(("wide", "col"), None),
        P(("wide", "col"), None, None, None),
        P(("wide", "col"), None),
        P(("wide", "col"), None, None, None),
        P(("wide", "col"), None),
        P(("wide", "col"), None),
        P(("wide", "col"), None, None),
    )
    out_specs = P(("wide", "col"), None)
    return jax.shard_map(
        on_device, mesh=mesh, in_specs=in_specs, out_specs=out_specs, check_vma=False
    )
```

```python
import functools

import jax
import jax.numpy as jnp
from jax import lax
from jax.experimental import pallas as pl
from jax.experimental.pallas import tpu as pltpu
from jax.sharding import PartitionSpec as P


REACH = 3
HIGHEST_PREC = lax.Precision.HIGHEST
SUB = 8
LANES = 128


def send(block, axis, route):
    return lax.ppermute(block, axis, route)


def along(block, axis, distance):
    count = lax.axis_size(axis)
    return send(
        block, axis, [(i, i + distance) for i in range(count) if 0 <= i + distance < count]
    )


def swap(block, axis, bit):
    return send(block, axis, [(i, i ^ bit) for i in range(lax.axis_size(axis))])


def outward(block, axis):
    count = lax.axis_size(axis)
    route = [(i, i + 1 if i % 2 else i - 1) for i in range(count)]
    return send(block, axis, [(s, t) for s, t in route if 0 <= t < count])


def relay(block, axis):
    count = lax.axis_size(axis)
    route = [(i, i - 2 if i % 2 else i + 2) for i in range(count)]
    return send(block, axis, [(s, t) for s, t in route if 0 <= t < count])


def is_even(axis):
    return lax.axis_index(axis) % 2 == 0


def join_halves(block, axis, bit):
    mine = (lax.axis_index(axis) // bit) % 2
    other = swap(block, axis, bit)
    return jnp.where(
        mine == 0,
        jnp.concatenate([block, other], axis=0),
        jnp.concatenate([other, block], axis=0),
    )


def sum_stages():
    stages = []
    for axis in ("wide", "col"):
        size = lax.axis_size(axis)
        if size & (size - 1):
            raise ValueError("axis size")
        stages += [(axis, 1 << k) for k in range(size.bit_length() - 1)]
    return stages


SPLITS = 3


def split_bits():
    sides = [(lax.axis_index(axis) // bit) % 2 for axis, bit in sum_stages()[:SPLITS]]
    return jnp.stack(sides).astype(jnp.int32)


def halves(total, side):
    half = total.shape[0] // 2
    kept = pl.multiple_of(side * half, SUB)
    given = pl.multiple_of((1 - side) * half, SUB)
    return total[pl.ds(kept, half), :], total[pl.ds(given, half), :]


def split_kernel(bits, kept, received, kept_out, given_out, total, *, stage):
    total[...] = kept[...] + received[...]
    kept_out[...], given_out[...] = halves(total, bits[stage])


def sum_everywhere(kept, given, bits, splits):
    stages = sum_stages()
    for stage, (axis, bit) in enumerate(stages[:splits]):
        received = swap(given, axis, bit)
        if stage + 1 < splits:
            rows, width = kept.shape
            kept, given = call(
                functools.partial(split_kernel, stage=stage + 1),
                [((rows // 2, width), jnp.float32)] * 2,
                (0,),
                (bits, kept, received),
                [pltpu.VMEM((rows, width), jnp.float32)],
            )
        else:
            block = kept + received
    for axis, bit in stages[splits:]:
        block = block + swap(block, axis, bit)
    for axis, bit in reversed(stages[:splits]):
        block = join_halves(block, axis, bit)
    return block


def far_line(block, axis):
    rows = block.shape[0]
    pair = swap(block, axis, 1)
    both = jnp.concatenate([block, pair], axis=0)
    below = along(both, axis, 2)
    above = along(both, axis, -2)
    last = relay(jnp.where(is_even(axis), below[rows:], above[rows:]), axis)
    return [
        (block, 0),
        (pair, 0),
        (below, 0),
        (below, 1),
        (above, 0),
        (above, 1),
        (last, 0),
    ]


def line_slot(target, own):
    pair_step = target // 2 - own // 2
    other = (target + own) % 2
    return jnp.where(
        pair_step == 0,
        other,
        jnp.where(pair_step == -1, 2 + other, jnp.where(pair_step == 1, 4 + other, 6)),
    )


def near_slot(target, own):
    return jnp.where(target == own, 0, jnp.where(target // 2 == own // 2, 1, 2))


def short_wide():
    return lax.axis_size("wide") == REACH + 1


def far_row_slot(target, own, short):
    if short:
        same_pair = target // 2 == own // 2
        other = (target + own) % 2
        return jnp.where(same_pair, 0, 2) + other
    return line_slot(target, own)


def holds_outer(wide_pos):
    wide = lax.axis_size("wide")
    source = wide_pos - 1 if wide_pos % 2 == 0 else wide_pos + 1
    return 0 <= source < wide


def outer_send(block, step):
    cols = lax.axis_size("col")
    route = []
    for w in range(lax.axis_size("wide")):
        if not holds_outer(w):
            continue
        for c in range(cols):
            target = step(c)
            if 0 <= target < cols:
                route.append((w * cols + c, w * cols + target))
    return lax.ppermute(block, ("wide", "col"), route)


def gather_windows(zb, coef):
    rank = coef.shape[0]
    xc = swap(coef, "col", 1)
    xn = swap(zb, "col", 1)
    yn = outward(zb, "wide")
    pair = jnp.concatenate([coef, xc], axis=0)
    zu = along(pair, "col", 2)
    zd = along(pair, "col", -2)
    xo = outer_send(yn, lambda c: c ^ 1)
    zn = relay(xn, "col")
    third = relay(jnp.where(is_even("col"), zu[rank:], zd[rank:]), "col")
    zo = outer_send(xo, lambda c: c - 2 if c % 2 else c + 2)
    near = {(0, 0): zb, (0, 1): xn, (0, 2): zn, (2, 0): yn, (2, 1): xo, (2, 2): zo}
    for col_slot in range(3):
        near[1, col_slot] = swap(near[0, col_slot], "wide", 1)
    own_line = [(coef, 0), (xc, 0), (zu, 0), (zu, 1), (zd, 0), (zd, 1), (third, 0)]
    far = {}
    if short_wide():
        yp = swap(pair, "wide", 2)
        quad = jnp.concatenate([zu, zd], axis=0)
        yq = swap(quad, "wide", 2)
        yt = swap(third, "wide", 2)
        ca = swap(jnp.concatenate([pair, yp], axis=0), "wide", 1)
        cq = swap(quad, "wide", 1)
        cb = swap(jnp.concatenate([third, yq, yt], axis=0), "wide", 1)
        y_line = [(yp, 0), (yp, 1), (yq, 0), (yq, 1), (yq, 2), (yq, 3), (yt, 0)]
        c_line = [(ca, 0), (ca, 1), (cq, 0), (cq, 1), (cq, 2), (cq, 3), (cb, 0)]
        cy_line = [(ca, 2), (ca, 3), (cb, 1), (cb, 2), (cb, 3), (cb, 4), (cb, 5)]
        for wide_slot, line in enumerate((own_line, c_line, y_line, cy_line)):
            for col_slot, piece in enumerate(line):
                far[wide_slot, col_slot] = piece
    else:
        stacked = jnp.concatenate([coef, xc, zu, zd, third], axis=0)
        for wide_slot, (array, part) in enumerate(far_line(stacked, "wide")):
            for col_slot in range(2 * REACH + 1):
                far[wide_slot, col_slot] = (array, part * (2 * REACH + 1) + col_slot)
    return near, far


def mm(left, right, contract=(1, 0)):
    return lax.dot_general(
        left,
        right,
        (((contract[0],), (contract[1],)), ((), ())),
        precision=HIGHEST_PREC,
        preferred_element_type=jnp.float32,
    )


def mm_bf16(left, right, contract=(1, 0)):
    return lax.dot_general(
        left,
        right,
        (((contract[0],), (contract[1],)), ((), ())),
        preferred_element_type=jnp.float32,
    )


def row_across(tile, row):
    return jnp.broadcast_to(tile[row : row + 1, :], tile.shape)


def eliminate_strip(strip, pivots):
    rows = lax.broadcasted_iota(jnp.int32, (SUB, LANES), 0)
    columns = [
        jnp.broadcast_to(strip[:, pivots + j : pivots + j + 1], (SUB, LANES)) for j in range(SUB)
    ]
    tiles = [strip[:, t : t + LANES] for t in range(0, strip.shape[1], LANES)]
    for i in range(SUB):
        pivot = row_across(columns[i], i)
        products = [columns[i] * row_across(columns[j], i) for j in range(i + 1, SUB)]
        inverse_root = lax.rsqrt(pivot)
        inverse = inverse_root * inverse_root
        for j in range(i + 1, SUB):
            columns[j] = columns[j] - products[j - i - 1] * inverse
        factor = jnp.where(rows > i, columns[i] * inverse_root, 0.0)
        for t in range(len(tiles)):
            scaled = row_across(tiles[t], i) * inverse_root
            tiles[t] = jnp.where(rows == i, scaled, tiles[t] - factor * scaled)
    return jnp.concatenate(tiles, axis=1)


def factorize(*works):
    size = works[0].shape[0]
    unit = (
        lax.broadcasted_iota(jnp.int32, (size, size), 0)
        == lax.broadcasted_iota(jnp.int32, (size, size), 1)
    ).astype(jnp.float32)
    for work in works:
        work[:, size:] = unit

    def panel(step, carry):
        first = pl.multiple_of(step * LANES, LANES)
        lanes = pl.ds(first, size + LANES)
        count = LANES // SUB
        panels = [[w[pl.ds(first + k * SUB, SUB), lanes] for k in range(count)] for w in works]
        for k in range(count):
            for work, strips in zip(works, panels):
                strips[k] = eliminate_strip(strips[k], k * SUB)
                work[pl.ds(first + k * SUB, SUB), lanes] = strips[k]
            turned = [strips[k][:, :LANES].T for strips in panels]
            for q in range(k + 1, count):
                for strips, turn in zip(panels, turned):
                    block = turn[q * SUB : (q + 1) * SUB, :]
                    rest = strips[q]
                    for i in range(SUB):
                        rest = rest - jnp.broadcast_to(
                            block[:, i : i + 1], rest.shape
                        ) * jnp.broadcast_to(strips[k][i : i + 1, :], rest.shape)
                    strips[q] = rest

        def below(part, inner):
            low = pl.multiple_of(part * LANES, LANES)
            for work in works:
                done = work[pl.ds(first, LANES), lanes]
                turned = work[pl.ds(first, LANES), pl.ds(low, LANES)]
                update = mm(turned, done, (0, 0))
                work[pl.ds(low, LANES), lanes] = work[pl.ds(low, LANES), lanes] - update
            return inner

        lax.fori_loop(step + 1, size // LANES, below, 0)
        return carry

    lax.fori_loop(0, size // LANES, panel, 0)


def upper(work):
    size = work.shape[0]
    keep = lax.broadcasted_iota(jnp.int32, (size, size), 1) >= lax.broadcasted_iota(
        jnp.int32, (size, size), 0
    )
    return jnp.where(keep, work[:, :size], 0.0)


def window_rows(padded, start, size):
    base = pl.multiple_of((start // SUB) * SUB, SUB)
    taken = padded[pl.ds(base, size + SUB), :]
    return pltpu.roll(taken, (size + SUB - start % SUB) % (size + SUB), 0)[:size]


def add_window(padded, start, addend):
    size = addend.shape[0]
    base = pl.multiple_of((start // SUB) * SUB, SUB)
    longer = jnp.concatenate([addend, jnp.zeros((SUB, addend.shape[1]), addend.dtype)], axis=0)
    span = pl.ds(base, size + SUB)
    padded[span, :] = padded[span, :] + pltpu.roll(longer, start % SUB, 0)


def row_parts(rows, size, do):
    def part(index, carry):
        do(pl.ds(pl.multiple_of(index * size, size), size))
        return carry

    lax.fori_loop(0, rows // size, part, 0)


def mm_into(out, left, right, contract):
    def part(at):
        rows = left[:, at] if contract[0] == 0 else left[at, :]
        out[at, :] = mm(rows, right[...], contract)

    row_parts(out.shape[0], LANES, part)


def write_vector(starts, vb_out, top_out, bottom_out, padded):
    rows = vb_out.shape[0]

    def cast(at):
        vb_out[at, :] = padded[at, :].astype(jnp.bfloat16)

    row_parts(rows, 2 * LANES, cast)
    padded[rows:, :] = jnp.zeros((SUB, padded.shape[1]), padded.dtype)
    margin = top_out.shape[0]
    top_out[...] = window_rows(padded, starts[0, 0], margin).astype(jnp.bfloat16)
    bottom_out[...] = window_rows(padded, starts[0, 1], margin).astype(jnp.bfloat16)


def gram_kernel(bits, rhs, kept_out, given_out, total):
    total[...] = jnp.zeros(total.shape, jnp.float32)

    def add(at):
        total[...] += mm(rhs[at, :], rhs[at, :], (0, 0))

    row_parts(rhs.shape[0], total.shape[0], add)
    kept_out[...], given_out[...] = halves(total, bits[0])


def first_kernel(starts, gram, rhs, v_out, vb_out, top_out, bottom_out, u_out, work, padded):
    size = gram.shape[0]
    work[:, :size] = gram[...]
    factorize(work)

    def solve(at):
        v = mm(rhs[at, :], work[:, size:], (1, 1))
        v_out[at, :] = v
        padded[at, :] = v

    row_parts(rhs.shape[0], size, solve)
    write_vector(starts, vb_out, top_out, bottom_out, padded)
    u_out[...] = upper(work)


def second_kernel(
    starts, sums, u0, v1, w, vb_out, top_out, bottom_out, k_inv_out, t1_out, work, other, padded
):
    size = u0.shape[0]
    h = sums.at[:, :size]
    mm_into(t1_out, h, h, (0, 0))
    work[:, :size] = sums[:, size:] - t1_out[...]
    other[:, :size] = sums[:, size:]
    factorize(work, other)

    def solve(at):
        rest = w[at, :] - mm(v1[at, :], sums[:, :size])
        padded[at, :] = mm(rest, work[:, size:], (1, 1))

    row_parts(w.shape[0], size, solve)
    write_vector(starts, vb_out, top_out, bottom_out, padded)
    k_inv_out[...] = other[:, size:]
    right = work.at[:, :size]
    mm_into(right, h, u0, (0, 0))
    mm_into(t1_out, k_inv_out, right, (1, 0))


def last_kernel(sums, u0, k_inv, t1, z1, z2, out, work, weights, cross, temp, other):
    size = u0.shape[0]
    mm_into(cross, k_inv, sums.at[:, size : 2 * size], (1, 0))
    mm_into(temp, cross, cross, (0, 0))
    work[:, :size] = sums[:, 2 * size :] - temp[...]
    factorize(work)
    inverse = work.at[:, size:]
    mm_into(temp, sums.at[:, :size], u0, (0, 0))
    mm_into(other, cross, t1, (0, 0))
    temp[...] = temp[...] - other[...]
    mm_into(other, inverse, temp, (1, 0))
    mm_into(weights.at[size:, :], inverse, other, (0, 0))
    mm_into(temp, cross, weights.at[size:, :], (1, 0))
    temp[...] = t1[...] - temp[...]
    mm_into(weights.at[:size, :], k_inv, temp, (0, 0))

    def rows_out(part, carry):
        at = pl.ds(pl.multiple_of(part * size, size), size)
        out[at, :] = mm(z1[at, :], weights[:size, :]) + mm(z2[at, :], weights[size:, :])
        return carry

    lax.fori_loop(0, out.shape[0] // size, rows_out, 0)


def edge_kernel(inverse, vb, before, after, low_out, high_out):
    margin = before.shape[0]
    rows = vb.shape[0]

    def of(rows_at):
        return (
            mm_bf16(inverse[0, rows_at, margin : margin + rows], vb[...])
            + mm_bf16(inverse[0, rows_at, :margin], before[...])
            + mm_bf16(inverse[0, rows_at, margin + rows :], after[...])
        )

    low_out[...] = of(slice(0, margin)).astype(low_out.dtype)
    high_out[...] = of(slice(margin + rows, None)).astype(high_out.dtype)


def middle_kernel(inverse, vb, before, after, mid_out):
    margin = before.shape[0]
    rows = vb.shape[0]

    def part(index, carry):
        to = pl.ds(pl.multiple_of(index * margin, margin), margin)
        at = pl.ds(pl.multiple_of((index + 1) * margin, margin), margin)
        mid_out[to, :] = (
            mm_bf16(inverse[0, at, margin : margin + rows], vb[...])
            + mm_bf16(inverse[0, at, :margin], before[...])
            + mm_bf16(inverse[0, at, margin + rows :], after[...])
        )
        return carry

    lax.fori_loop(0, rows // margin, part, 0)


def place_kernel(starts, mid, from_next, from_prev, basis, z_out, zb_out, coef_out, padded):
    rows = mid.shape[0]
    margin = from_next.shape[0]

    def start(at):
        padded[at, :] = mid[at, :]

    row_parts(rows, margin, start)
    padded[rows:, :] = jnp.zeros((SUB, mid.shape[1]), jnp.float32)
    add_window(padded, starts[0, 1], from_next[...].astype(jnp.float32))
    add_window(padded, starts[0, 0], from_prev[...].astype(jnp.float32))

    def finish(at):
        z_out[at, :] = padded[at, :]
        zb_out[at, :] = padded[at, :].astype(jnp.bfloat16)

    row_parts(rows, margin, finish)
    rank = coef_out.shape[0]
    padded[:rank, :] = jnp.zeros((rank, mid.shape[1]), jnp.float32)

    def add(at):
        padded[:rank, :] += mm_bf16(basis[at, :], zb_out[at, :], (0, 0))

    row_parts(rows, margin, add)
    coef_out[...] = padded[:rank, :].astype(jnp.bfloat16)


def in_vmem():
    return pl.BlockSpec(memory_space=pltpu.VMEM)


def in_smem():
    return pl.BlockSpec(memory_space=pltpu.SMEM)


def call(kernel, shapes, smem, args, scratch=(), vmem=None, anywhere=()):
    specs = [in_smem() if i in smem else in_vmem() for i in range(len(args))]
    args = list(args)
    for i in anywhere:
        specs[i] = pl.BlockSpec(memory_space=pltpu.HBM)
        args[i] = pltpu.with_memory_space_constraint(args[i], pltpu.HBM)
    outs = tuple(jax.ShapeDtypeStruct(shape, dtype) for shape, dtype in shapes)
    return pl.pallas_call(
        kernel,
        out_shape=outs,
        in_specs=specs,
        out_specs=tuple(in_vmem() for _ in outs),
        scratch_shapes=list(scratch),
        compiler_params=pltpu.CompilerParams(vmem_limit_bytes=vmem or SMALL_VMEM),
    )(*args)


NEAR_SIDE = 3
FAR_GROUP = 4
FIELD_VMEM = 22 * 1024 * 1024
SMALL_VMEM = 16 * 1024 * 1024


def block_copy(near_at, first, i, blocks_hbm, blocks, sems):
    slot = jnp.maximum(near_at[first + i], 0)
    return pltpu.make_async_copy(blocks_hbm.at[0, slot], blocks.at[i], sems.at[i])


def add_near(near_at, first, stack, blocks_hbm, blocks, sems, w_out):
    rows = w_out.shape[0]

    def add(i, carry):
        block_copy(near_at, first, i, blocks_hbm, blocks, sems).wait()

        @pl.when(near_at[first + i] >= 0)
        def _():
            at = pl.multiple_of(i * rows, rows)
            w_out[...] += mm_bf16(blocks[i], stack[pl.ds(at, rows), :])

        return carry

    lax.fori_loop(0, blocks.shape[0], add, 0)


NEAR_ORDER = (0, 3, 6, 1, 4, 7, 2, 5, 8)
EARLY = 6


def stack_pieces(pieces, stack):
    rows = pieces[0].shape[0]
    for i, piece in enumerate(pieces):

        def copy(at, i=i, piece=piece):
            to = pl.ds(pl.multiple_of(i * rows + at.start, LANES), at.size)
            stack[to, :] = piece[at, :]

        row_parts(rows, 2 * LANES, copy)


def early_kernel(near_at, *refs):
    *pieces, self_hbm, blocks_hbm, w_out, stack, blocks, sems = refs
    pltpu.make_async_copy(self_hbm, blocks.at[0], sems.at[0]).start()
    for i in range(1, EARLY):
        block_copy(near_at, 0, i, blocks_hbm, blocks, sems).start()

    def clear(at):
        w_out[at, :] = jnp.zeros((at.size, w_out.shape[1]), jnp.float32)

    row_parts(w_out.shape[0], LANES, clear)
    stack_pieces(pieces, stack)
    add_near(near_at, 0, stack, blocks_hbm, blocks, sems, w_out)


def late_kernel(near_at, far_at, bits, *refs, far_places, n_far, n_vectors):
    it = iter(refs)
    pieces = [next(it) for _ in range(NEAR_SIDE)]
    far_arrays = [next(it) for _ in range(n_far)]
    w_in, blocks_hbm, couplings_hbm, basis_hbm = (next(it) for _ in range(4))
    vectors_hbm = [next(it) for _ in range(n_vectors)]
    w_out, kept_out, given_out, far, total, stack = (next(it) for _ in range(6))
    blocks, sems, couplings, group_sems, fixed_sems, basis, *vectors = it
    slots = couplings.shape[0]
    groups = far_at[slots]

    def group_copy(group):
        at = pl.ds(group * FAR_GROUP, FAR_GROUP)
        return pltpu.make_async_copy(
            couplings_hbm.at[0, at], couplings.at[at], group_sems.at[group]
        )

    def start_group(group, carry):
        group_copy(group).start()
        return carry

    lax.fori_loop(0, groups, start_group, 0)
    fixed = [
        pltpu.make_async_copy(source, target, fixed_sems.at[i])
        for i, (source, target) in enumerate(zip([basis_hbm] + vectors_hbm, [basis] + vectors))
    ]
    fixed[0].start()
    for i in range(NEAR_SIDE):
        block_copy(near_at, EARLY, i, blocks_hbm, blocks, sems).start()
    for copy in fixed[1:]:
        copy.start()
    stack_pieces(pieces, stack)
    rank = basis.shape[1]
    width = w_out.shape[1]
    for i, (array, part) in enumerate(far_places):

        def copy(at, i=i, array=array, part=part):
            to = pl.ds(pl.multiple_of(i * rank + at.start, LANES), at.size)
            source = pl.ds(pl.multiple_of(part * rank + at.start, LANES), at.size)
            far[to, :] = far_arrays[array][source, :]

        row_parts(rank, LANES, copy)

    last = len(far_places) * rank
    far[last:, :] = jnp.zeros((rank, width), far.dtype)
    total[...] = jnp.zeros(total.shape, jnp.float32)

    def add_group(group, carry):
        def product(slot):
            at = pl.multiple_of(far_at[slot] * rank, rank)
            return mm_bf16(couplings[slot], far[pl.ds(at, rank), :])

        group_copy(group).wait()
        first = group * FAR_GROUP
        added = product(first)
        for k in range(1, FAR_GROUP):
            added = added + product(first + k)
        total[:, :width] += added
        return carry

    lax.fori_loop(0, groups, add_group, 0)
    fixed[0].wait()
    far[:rank, :] = total[:, :width].astype(jnp.bfloat16)

    def add_basis(at):
        w_out[at, :] = w_in[at, :] + mm_bf16(basis[at, :], far[:rank, :])

    row_parts(w_out.shape[0], width, add_basis)
    add_near(near_at, EARLY, stack, blocks_hbm, blocks, sems, w_out)
    for copy in fixed[1:]:
        copy.wait()
    total[:, :width] = jnp.zeros((rank, width), jnp.float32)

    def add_grams(at):
        for i, vector in enumerate(vectors + [w_out]):
            total[:, i * width : (i + 1) * width] += mm(vector[at, :], w_out[at, :], (0, 0))

    row_parts(w_out.shape[0], width, add_grams)
    kept_out[...], given_out[...] = halves(total, bits[0])


def window_tables(near_ids, far_ids, far_slots):
    cols = lax.axis_size("col")
    wide_pos, col_pos = lax.axis_index("wide"), lax.axis_index("col")
    ids = near_ids[0]
    safe = jnp.maximum(ids, 0)
    at = near_slot(safe // cols, wide_pos) * NEAR_SIDE + near_slot(safe % cols, col_pos)
    positions = jnp.array(NEAR_ORDER)
    hit = (at[None, :] == positions[:, None]) & (ids >= 0)[None, :]
    near_at = jnp.max(jnp.where(hit, jnp.arange(ids.shape[0])[None, :], -1), axis=1)
    near_at = jnp.where(positions == 0, 0, near_at)
    ids = far_ids[0]
    safe = jnp.maximum(ids, 0)
    row = far_row_slot(safe // cols, wide_pos, short_wide())
    at = row * (2 * REACH + 1) + line_slot(safe % cols, col_pos)
    live = ids >= 0
    groups = (jnp.sum(live.astype(jnp.int32)) + FAR_GROUP - 1) // FAR_GROUP
    far_at = jnp.concatenate([jnp.where(live, at, far_slots), groups[None]])
    return near_at.astype(jnp.int32), far_at.astype(jnp.int32)


def far_slot_count():
    rows = REACH + 1 if short_wide() else 2 * REACH + 1
    return rows * (2 * REACH + 1)


def operate(zb, coef, basis, self_block, near_block, tables, couplings, bits, vectors):
    near, far = gather_windows(zb, coef)
    near_at, far_at = tables
    rows, width = zb.shape
    rank = basis.shape[1]
    whole = ((rows, width), jnp.float32)
    pieces = [near[divmod(position, NEAR_SIDE)] for position in NEAR_ORDER]
    early = pieces[:EARLY]
    (w,) = call(
        early_kernel,
        [whole],
        (0,),
        (near_at, *early, self_block, near_block),
        [
            pltpu.VMEM((EARLY * rows, width), jnp.bfloat16),
            pltpu.VMEM((EARLY, rows, rows), near_block.dtype),
            pltpu.SemaphoreType.DMA((EARLY,)),
        ],
        vmem=FIELD_VMEM,
        anywhere=(len(early) + 1, len(early) + 2),
    )
    arrays, places = [], []
    for key in sorted(far):
        array, part = far[key]
        known = [i for i, other in enumerate(arrays) if other is array]
        if not known:
            arrays.append(array)
        places.append((known[0] if known else len(arrays) - 1, part))
    sums_width = (len(vectors) + 1) * width
    half = ((width // 2, sums_width), jnp.float32)
    return call(
        functools.partial(
            late_kernel,
            far_places=tuple(places),
            n_far=len(arrays),
            n_vectors=len(vectors),
        ),
        [whole, half, half],
        (0, 1, 2),
        (
            near_at,
            far_at,
            bits,
            *pieces[len(early) :],
            *arrays,
            w,
            near_block,
            couplings,
            basis,
            *vectors,
        ),
        [
            pltpu.VMEM(((len(places) + 1) * rank, width), jnp.bfloat16),
            pltpu.VMEM((width, sums_width), jnp.float32),
            pltpu.VMEM((NEAR_SIDE * rows, width), jnp.bfloat16),
            pltpu.VMEM((NEAR_SIDE, rows, rows), near_block.dtype),
            pltpu.SemaphoreType.DMA((NEAR_SIDE,)),
            pltpu.VMEM(couplings.shape[1:], couplings.dtype),
            pltpu.SemaphoreType.DMA((couplings.shape[1] // FAR_GROUP,)),
            pltpu.SemaphoreType.DMA((1 + len(vectors),)),
            pltpu.VMEM(basis.shape, basis.dtype),
        ]
        + [pltpu.VMEM(vector.shape, vector.dtype) for vector in vectors],
        vmem=FIELD_VMEM if short_wide() else 2 * FIELD_VMEM,
        anywhere=tuple(3 + NEAR_SIDE + len(arrays) + k for k in range(1, 4 + len(vectors))),
    )


def precondition(vb, top, bottom, starts, schwarz_inverse, basis):
    rows, width = vb.shape
    margin = top.shape[0]
    rank = basis.shape[1]
    before = along(bottom, "col", 1)
    after = along(top, "col", -1)
    args = (schwarz_inverse, vb, before, after)
    edge = ((margin, width), jnp.float32)
    low, high = call(edge_kernel, [edge, edge], (), args)
    from_next = along(low, "col", -1)
    from_prev = along(high, "col", 1)
    (mid,) = call(middle_kernel, [((rows, width), jnp.float32)], (), args)
    return call(
        place_kernel,
        [((rows, width), jnp.float32), ((rows, width), jnp.bfloat16), ((rank, width), jnp.bfloat16)],
        (0,),
        (starts, mid, from_next, from_prev, basis),
        [pltpu.VMEM((rows + SUB, width), jnp.float32)],
    )


def on_device(
    rhs,
    basis,
    self_block,
    near_block,
    near_ids,
    couplings,
    far_ids,
    intersection_start,
    schwarz_inverse,
):
    rows, width = rhs.shape
    margin = (schwarz_inverse.shape[1] - rows) // 2
    square = ((width, width), jnp.float32)
    whole = ((rows, width), jnp.float32)
    sent = [
        ((rows, width), jnp.bfloat16),
        ((margin, width), jnp.bfloat16),
        ((margin, width), jnp.bfloat16),
    ]
    work = [pltpu.VMEM((width, 2 * width), jnp.float32)]
    padded = [pltpu.VMEM((rows + SUB, width), jnp.float32)]
    bits = split_bits()
    tables = window_tables(near_ids, far_ids, far_slot_count())
    fixed = (basis, self_block, near_block, tables, couplings, bits)

    half = ((width // 2, width), jnp.float32)
    kept0, given0 = call(
        gram_kernel, [half, half], (0,), (bits, rhs), [pltpu.VMEM((width, width), jnp.float32)]
    )
    gram0 = sum_everywhere(kept0, given0, bits, 2)
    v1, vb1, top1, bottom1, u0 = call(
        first_kernel,
        [whole] + sent + [square],
        (0,),
        (intersection_start, gram0, rhs),
        work + padded,
    )
    z1, zb1, coef1 = precondition(
        vb1, top1, bottom1, intersection_start, schwarz_inverse, basis
    )
    w1, kept1, given1 = operate(zb1, coef1, *fixed, (v1,))
    sums1 = sum_everywhere(kept1, given1, bits, SPLITS)
    vb2, top2, bottom2, k_inv, t1 = call(
        second_kernel,
        sent + [square, square],
        (0,),
        (intersection_start, sums1, u0, v1, w1),
        work + work + padded,
    )
    z2, zb2, coef2 = precondition(
        vb2, top2, bottom2, intersection_start, schwarz_inverse, basis
    )
    _, kept2, given2 = operate(zb2, coef2, *fixed, (v1, w1))
    sums2 = sum_everywhere(kept2, given2, bits, SPLITS)
    (solution_rows,) = call(
        last_kernel,
        [whole],
        (),
        (sums2, u0, k_inv, t1, z1, z2),
        work
        + [pltpu.VMEM((2 * width, width), jnp.float32)]
        + [pltpu.VMEM((width, width), jnp.float32)] * 3,
    )
    return solution_rows


def solution(mesh):
    in_specs = (
        P(("wide", "col"), None),
        P(("wide", "col"), None),
        P(("wide", "col"), None),
        P(("wide", "col"), None, None, None),
        P(("wide", "col"), None),
        P(("wide", "col"), None, None, None),
        P(("wide", "col"), None),
        P(("wide", "col"), None),
        P(("wide", "col"), None, None),
    )
    out_specs = P(("wide", "col"), None)
    return jax.shard_map(
        on_device, mesh=mesh, in_specs=in_specs, out_specs=out_specs, check_vma=False
    )
```
